256 devices in a mesh: gx: 32 (over y_hi, z, core), gy: 8 (over y_lo, x).
Axes of the slice: x: 4, y: 4 (y_hi: 2, y_lo: 2; y = y_hi * 2 + y_lo), z: 8, core: 2. Of those that a mesh axis runs over, the one named last changes fastest.
Arguments:
- adj_later: float32 [19, 256, 128, 256], P(None, 'gx', 'gy'), may hold values from -6 to 6
- saved_pops: bfloat16 [2, 19, 256, 128, 256], P(None, None, 'gx', 'gy'), may hold values from 0.015 to 0.49, as said below
- saved_scale: float32 [2, 19, 256, 128, 2], P(None, None, 'gx', 'gy'), may hold values from 0.7 to 1.4
- solid: int32 [256, 128, 256], P('gx', 'gy'), may hold values 0 or 1
- seed_values: float32 [32768, 19], P(('gx', 'gy')), may hold values from -12 to 12
- seed_contact: int32 [32768, 1], P(('gx', 'gy')), may hold values from 0 to 8; in each aligned block of 128 rows (0 to 127, 128 to 255, ...) at most 32 rows name the same one
- seed_cell: int32 [32768], P(('gx', 'gy')), may hold values from 0 to 32767
Outputs:
- adj_initial: float32 [19, 256, 128, 256], P(None, 'gx', 'gy')
- adj_middle: float32 [19, 256, 128, 256], P(None, 'gx', 'gy')
The draws below stay inside these ranges and needn't reach their ends.
Inputs may be any that keep to these rules, and one draw needn't show every extreme that they name: `saved_pops`: each saved population is its lattice weight w_i times a factor between 0.55 and 1.45. `seed_contact`: among the items held by one device no contact code appears more than 32 times; some code reaches 32 on some device.
All inputs are finite; a program needn't handle non-finite values. No bound on the sum of `solid` on one device may be relied on, other than what follows from the above.
Results may differ from the reference program's by a relative error of at most 0.0003.
Values sent between devices are 32-bit elements; how exact they have to be, the bound alone decides.
No kernel may reach another device: no remote copies, remote signals or barrier semaphores. Data moves between devices by JAX's collectives and lax.ppermute only.
A program may use at most 128 MiB of HBM per device.

```python
import math
import jax
import jax.numpy as jnp
import numpy as np
from jax import lax

CX = 8
CY = 16
CZ = 256
ZB = 128
SURF_DEV = 128
CAP = 32
NX = 256
NY = 128
NZ = 256
NZB = 2
SURF_TOT = 32768
N_GX = 32
N_GY = 8


def draw_saved_pops(key, part):
    weights = jnp.array([1.0 / 3.0] + [1.0 / 18.0] * 6 + [1.0 / 36.0] * 12, jnp.float32).reshape(1, 19, 1, 1, 1)
    array_shape = (2, 19, NX, NY, NZ)
    jitter = jnp.clip(0.15 * jax.random.normal(key, array_shape, jnp.float32), -0.45, 0.45)
    return (weights * (1.0 + jitter)).astype(jnp.bfloat16)


def set_ends(entries, key, least, largest):
    extent = entries.shape
    index_at = [jax.random.randint(jax.random.fold_in(key, axis), (), 0, extent[axis]) for axis in range(len(extent))]
    entries = entries.at[tuple(index_at)].set(least)
    longest = extent.index(max(extent))
    index_at[longest] = (index_at[longest] + 1) % extent[longest]
    return entries.at[tuple(index_at)].set(largest)


def block_levels(stream_key, extent, pieces, smallest, top_value):
    def one(dim, parts):
        heights = jax.random.uniform(jax.random.fold_in(jax.random.fold_in(stream_key, 6), dim), (parts,), jnp.float32, smallest / len(pieces), top_value / len(pieces))
        return jnp.repeat(jnp.exp(heights), extent[dim] // parts).reshape((-1,) + (1,) * (len(extent) - dim - 1))

    loudness = one(*pieces[0])
    for cut in pieces[1:]:
        loudness = loudness * one(*cut)
    return loudness


def routed_block(rng, own, number, rows, count, top, limit, skew):
    sequence = jax.random.permutation(rng, count)
    packed, ordinary = portions_of(count, rows * top, limit, skew, True), portions_of(count, rows * top, limit, skew, False)
    places = jnp.arange(count)

    def named(tallies, turn):
        used = int((tallies > 0).sum())
        fixed = max(1, used // 4)
        moved = fixed + (places - fixed + turn * (used - fixed)) % max(1, count - fixed)
        return jnp.zeros((count,), jnp.int32).at[sequence[jnp.where(places < fixed, places, moved)]].set(jnp.asarray(tallies, jnp.int32))

    tallies = jnp.where(number % 4 == 0, named(packed, number // 4), named(ordinary, number - number // 4 - 1))
    mixed = jax.random.permutation(jax.random.fold_in(own, 3), count)
    source_of, sink = mixed[0:count // 2 * 2:2], mixed[1:count // 2 * 2:2]
    slack = jnp.minimum(tallies[source_of] - 1, limit - tallies[sink]) // 2
    slack = jnp.where((source_of == sequence[0]) | (sink == sequence[0]) | (tallies[sink] == 0), 0, jnp.maximum(slack, 0))
    moved = jax.random.randint(jax.random.fold_in(own, 4), (count // 2,), 0, 1 << 20) % (slack + 1)
    tallies = tallies.at[source_of].add(-moved).at[sink].add(moved)
    members = jnp.searchsorted(jnp.cumsum(tallies), jnp.arange(rows * top), side="right").astype(jnp.int32)
    grid = members.reshape(top, rows).T
    grid = grid[jax.random.permutation(jax.random.fold_in(own, 1), rows)]
    turn = jax.random.randint(jax.random.fold_in(own, 2), (rows, 1), 0, top)
    return jnp.take_along_axis(grid, (jnp.arange(top)[None, :] + turn) % top, axis=1)


def portions_of(count, total, most, lean, full):
    portions = [(1 << 20) // math.isqrt(grade ** lean) + 1 for grade in range(1, count + 1)]
    largest = most if full else min(most, max(-(-total // count), total * portions[0] // sum(portions)))
    least = 1 if total - largest >= count - 1 else 0
    given, surplus = [largest] + [least] * (count - 1), total - largest - least * (count - 1)
    while surplus > 0:
        movable = [i for i in range(1, count) if given[i] < largest] or [i for i in range(1, count) if given[i] < most]
        pool, budget = sum([portions[i] for i in movable]), surplus
        for i in movable:
            more = min(most - given[i], max(1, budget * portions[i] // pool), surplus)
            given[i] = given[i] + more
            surplus = surplus - more
    return np.array(given)


def gaussian(rng, shape, deviation, bound, pieces=(), kind=jnp.bfloat16):
    drawn = deviation * jax.random.normal(rng, shape, jnp.float32)
    if pieces:
        drawn = drawn * block_levels(rng, shape, pieces, -0.22, 0.18)
    return jnp.clip(drawn, -bound, bound).astype(kind)


def setup_inputs(seed: int = 0) -> dict:
    key_list = jax.random.split(jax.random.key(seed), 8)
    adj_later = gaussian(key_list[0], (19, NX, NY, NZ), 1.0, 6.0, ((1, 32), (2, 8)), jnp.float32)
    saved_pops = draw_saved_pops(jax.random.fold_in(key_list[7], 71), 0)
    saved_scale = jnp.clip(jnp.exp(math.log(1.4) - 0.6931472 * jax.random.uniform(key_list[2], (2, 19, NX, NY, NZB), jnp.float32) ** block_levels(key_list[2], (2, 19, NX, NY, NZB), ((2, 32), (3, 8)), -0.2, 0.2)), 0.7, 1.4)
    solid = set_ends((jax.random.randint(key_list[3], (NX, NY, NZ), 0, 5) < 1).astype(jnp.int32), jax.random.fold_in(key_list[3], 1), 0, 1)
    seed_values = gaussian(key_list[4], (SURF_TOT, 19), 3.0, 12.0, ((0, 256),), jnp.float32)
    seed_contact_keys = jax.random.split(jax.random.fold_in(key_list[5], 1), SURF_TOT // SURF_DEV)
    seed_contact_turns = jax.random.permutation(jax.random.fold_in(key_list[5], 3), SURF_TOT // SURF_DEV)
    seed_contact = jax.vmap(lambda own, number: routed_block(jax.random.fold_in(key_list[5], 2), own, number, SURF_DEV, 9, 1, CAP, 2))(seed_contact_keys, seed_contact_turns).reshape((SURF_TOT, 1))
    seed_cell = set_ends(jax.random.randint(key_list[6], (SURF_TOT,), 0, CX * CY * CZ), jax.random.fold_in(key_list[6], 1), 0, (CX * CY * CZ) - 1).astype(jnp.int32)
    return dict(adj_later=adj_later, saved_pops=saved_pops, saved_scale=saved_scale, solid=solid, seed_values=seed_values, seed_contact=seed_contact, seed_cell=seed_cell)


LATTICE = [(0, 0, 0), (1, 0, 0), (-1, 0, 0), (0, 1, 0), (0, -1, 0), (0, 0, 1), (0, 0, -1), (1, 1, 0), (-1, -1, 0), (1, -1, 0), (-1, 1, 0), (1, 0, 1), (-1, 0, -1), (1, 0, -1), (-1, 0, 1), (0, 1, 1), (0, -1, -1), (0, 1, -1), (0, -1, 1)]
OPPOSITE = [0, 2, 1, 4, 3, 6, 5, 8, 7, 10, 9, 12, 11, 14, 13, 16, 15, 18, 17]
LATTICE_WEIGHTS = [1.0 / 3.0] + [1.0 / 18.0] * 6 + [1.0 / 36.0] * 12
relaxation = 0.8

def collide(populations):
    lattice = jnp.array(LATTICE, jnp.float32).T
    weights = jnp.array(LATTICE_WEIGHTS, jnp.float32).reshape((19,) + (1,) * (populations.ndim - 1))
    density = lax.optimization_barrier(jnp.sum(populations, 0))
    momentum = jnp.einsum('ci,i...->c...', lattice, populations, precision=lax.Precision.HIGHEST)
    velocity = momentum / density
    projected = jnp.einsum('ci,c...->i...', lattice, velocity, precision=lax.Precision.HIGHEST)
    square = lax.optimization_barrier(jnp.sum(velocity * velocity, 0))
    equilibrium = weights * density * (1.0 + 3.0 * projected + 4.5 * projected * projected - 1.5 * square)
    return populations - (populations - equilibrium) / relaxation

def adjoint_collide(populations, adjoint, solid):
    unused, pull_back = jax.vjp(collide, populations)
    fluid_adjoint = pull_back(adjoint)[0]
    reversed_adjoint = jnp.stack([adjoint[other] for other in OPPOSITE])
    return jnp.where(solid[None] > 0, reversed_adjoint, fluid_adjoint)

def dequantize(quantized, scales):
    blocks = quantized.astype(jnp.float32).reshape(19, NX, NY, NZ // ZB, ZB)
    return (blocks * scales[..., None]).reshape(19, NX, NY, NZ)

def stream_back(adjoint):
    padded = jnp.pad(adjoint, ((0, 0), (1, 1), (1, 1), (1, 1)))
    slices = []
    for direction in range(19):
        step_x, step_y, step_z = LATTICE[direction]
        slices.append(padded[direction, 1 + step_x:1 + step_x + NX, 1 + step_y:1 + step_y + NY, 1 + step_z:1 + step_z + NZ])
    return jnp.stack(slices)

def adjoint_step(populations, adjoint, solid):
    read = jnp.moveaxis(stream_back(adjoint), 1, 0)
    pops_x = jnp.moveaxis(populations, 1, 0)
    result = lax.map(lambda group: adjoint_collide(group[0], group[1], group[2]), (pops_x, read, solid))
    return jnp.moveaxis(result, 0, 1)

def reference(adj_later, saved_pops, saved_scale, solid, seed_values, seed_contact, seed_cell):
    item_count = SURF_DEV * N_GX * N_GY
    source = jnp.arange(item_count, dtype=jnp.int32) // SURF_DEV
    contact = seed_contact[:, 0]
    target_x = source // N_GY + contact // 3 - 1
    target_y = source % N_GY + contact % 3 - 1
    valid = (target_x >= 0) & (target_x < N_GX) & (target_y >= 0) & (target_y < N_GY)
    global_x = jnp.clip(target_x, 0, N_GX - 1) * CX + seed_cell // (CY * CZ)
    global_y = jnp.clip(target_y, 0, N_GY - 1) * CY + seed_cell // CZ % CY
    global_z = seed_cell % CZ
    weighted = seed_values * valid[:, None].astype(jnp.float32)
    seed_field = jnp.zeros((19, NX, NY, NZ), jnp.float32).at[:, global_x, global_y, global_z].add(weighted.T)
    adjoint_end = adj_later + seed_field
    pops_late = dequantize(saved_pops[1], saved_scale[1])
    adj_middle = adjoint_step(pops_late, adjoint_end, solid)
    pops_early = dequantize(saved_pops[0], saved_scale[0])
    adj_initial = adjoint_step(pops_early, adj_middle, solid)
    return (adj_initial, adj_middle)
```

```python
import functools

import jax
import jax.numpy as jnp
from jax import lax
from jax.experimental import pallas as pl
from jax.experimental.pallas import tpu as pltpu
from jax.sharding import PartitionSpec as P

PAIRS = [
    (1, 2, (1, 0, 0)),
    (3, 4, (0, 1, 0)),
    (5, 6, (0, 0, 1)),
    (7, 8, (1, 1, 0)),
    (9, 10, (1, -1, 0)),
    (11, 12, (1, 0, 1)),
    (13, 14, (1, 0, -1)),
    (15, 16, (0, 1, 1)),
    (17, 18, (0, 1, -1)),
]
VEL = [(0, 0, 0)] * 19
for _p, _m, _c in PAIRS:
    VEL[_p] = _c
    VEL[_m] = tuple(-v for v in _c)
OPP = [0] * 19
for _p, _m, _c in PAIRS:
    OPP[_p], OPP[_m] = _m, _p
RELAX = 0.8
F32 = jnp.float32
BX, BY, BZ = 8, 16, 256
EX = 12
LIST = 32


def face_rows(axis, sign):
    near = [i for i in range(19) if VEL[i][axis] in (0, sign)]
    far = [i for i in range(19) if VEL[i][axis] == sign]
    return near, far


vmem = pl.BlockSpec(memory_space=pltpu.VMEM)
anyspace = pl.BlockSpec(memory_space=pl.ANY)


def in_vmem(x):
    return pltpu.with_memory_space_constraint(x, pltpu.VMEM)


def call(body, out_shape, in_specs, args, scratch=(), aliases=None, limit=20 << 20):
    single = not isinstance(out_shape, (tuple, list))
    outs = (out_shape,) if single else tuple(out_shape)
    out_specs = tuple(vmem if isinstance(o, type(pltpu.VMEM((8, 128), F32))) else anyspace for o in outs)
    res = pl.pallas_call(
        body,
        out_shape=outs,
        in_specs=in_specs,
        out_specs=out_specs,
        scratch_shapes=list(scratch),
        input_output_aliases=aliases or {},
        compiler_params=pltpu.CompilerParams(vmem_limit_bytes=limit),
    )(*args)
    return res[0] if single else res


def iota(shape, dim):
    return lax.broadcasted_iota(jnp.int32, shape, dim)


def group_items(values, contact, cell, low, mid, high, pay):
    code = contact[...]
    hot = (iota((16, 128), 0) == code).astype(jnp.bfloat16)
    before = (iota((128, 128), 0) < iota((128, 128), 1)).astype(jnp.bfloat16)
    counts = jnp.dot(hot, before, preferred_element_type=F32)
    rank = jnp.sum(jnp.where(iota((16, 128), 0) == code, counts, 0.0), axis=0, keepdims=True).astype(jnp.int32)
    third = (code >= 3).astype(jnp.int32) + (code >= 6).astype(jnp.int32)
    slot = third * 128 + (code - 3 * third) * LIST + rank
    pay[...] = jnp.zeros((24, 128), F32)
    pay[0:19, :] = values[...]
    pay[19:20, :] = cell[...].astype(F32)
    payload = pay[...]
    for part, out in enumerate((low, mid, high)):
        pick = (iota((128, 128), 0) + 128 * part == slot).astype(F32)
        out[...] = lax.dot_general(
            payload, pick, (((1,), (1,)), ((), ())), precision=lax.Precision.HIGHEST, preferred_element_type=F32
        )


def regroup(left, own, right, down, same, up):
    gx = lax.axis_index("gx")
    a = jnp.where(gx > 0, left[...], 0.0)
    b = own[...]
    c = jnp.where(gx < lax.axis_size("gx") - 1, right[...], 0.0)
    lane = iota((24, 128), 1)
    for j, out in enumerate((down, same, up)):
        ra = pltpu.roll(a, (-LIST * j) % 128, 1)
        rb = pltpu.roll(b, (LIST - LIST * j) % 128, 1)
        rc = pltpu.roll(c, (2 * LIST - LIST * j) % 128, 1)
        out[...] = jnp.where(
            lane < LIST, ra, jnp.where(lane < 2 * LIST, rb, jnp.where(lane < 3 * LIST, rc, 0.0))
        )


def velocities(pops, scale, adj, vel, ext, raw, sems, adj_sem):
    copies = []
    for s in range(2):
        for h in range(2):
            c = pltpu.make_async_copy(
                pops.at[s, :, pl.ds(4 * h, 4)], raw.at[s, :, pl.ds(4 * h, 4)], sems.at[2 * s + h]
            )
            c.start()
            copies.append(c)
    adj_copy = pltpu.make_async_copy(adj, ext.at[:, pl.ds(2, BX)], adj_sem)
    adj_copy.start()
    for s in range(2):
        for h in range(2):
            copies[2 * s + h].wait()

            def plane(x, carry, s=s):
                for b in range(2):
                    table = scale[s, x, pl.ds(b, BY, stride=2), :]

                    def pop(i):
                        f = raw[s, i, x, :, 128 * b : 128 * (b + 1)].astype(F32)
                        return f * jnp.broadcast_to(table[:, i : i + 1], (BY, 128))

                    density = pop(0)
                    mom = [None, None, None]
                    for plus, minus, c in PAIRS:
                        fp, fm = pop(plus), pop(minus)
                        density = density + (fp + fm)
                        d = fp - fm
                        for axis in range(3):
                            if c[axis]:
                                if mom[axis] is None:
                                    mom[axis] = d
                                elif c[axis] > 0:
                                    mom[axis] = mom[axis] + d
                                else:
                                    mom[axis] = mom[axis] - d
                    inv = 1.0 / density
                    for axis in range(3):
                        vel[s, axis, x, :, 128 * b : 128 * (b + 1)] = mom[axis] * inv
                return carry

            lax.fori_loop(4 * h, 4 * h + 4, plane, 0)
    adj_copy.wait()


def scatter(ext_in, vel, solid, down, same, up, ext, to_left, to_right, where_xy, where_z):
    del ext_in
    gy = lax.axis_index("gy")
    high, low = [], []
    for b, ref in enumerate((down, same, up)):
        block = ref[...]
        if b == 0:
            block = jnp.where(gy > 0, block, 0.0)
        elif b == 2:
            block = jnp.where(gy < lax.axis_size("gy") - 1, block, 0.0)
        cell = block[19:20, :].astype(jnp.int32)
        rows, height = cell // BZ, cell % BZ
        mask = (iota((128, 128), 0) == rows).astype(F32).astype(jnp.bfloat16)
        where_xy[:, 128 * b : 128 * (b + 1)] = mask
        hot = (iota((BZ, 128), 0) == height).astype(F32)
        spread = hot.T.astype(jnp.bfloat16)
        where_z[128 * b : 128 * (b + 1), :] = spread
        where_z[384 + 128 * b : 384 + 128 * (b + 1), :] = spread
        hi = block.astype(jnp.bfloat16).astype(F32)
        high.append(hi)
        low.append(block - hi)
    high = jnp.concatenate(high, axis=1)
    low = jnp.concatenate(low, axis=1)
    for i in range(19):
        rows = where_xy[...]
        left = rows * high[i : i + 1, :].astype(jnp.bfloat16)
        right = rows * low[i : i + 1, :].astype(jnp.bfloat16)
        both = jnp.concatenate([left, right], axis=1)
        field = jnp.dot(both, where_z[...], preferred_element_type=F32)
        ext[i, 2 : 2 + BX] = ext[i, 2 : 2 + BX] + field.reshape(BX, BY, BZ)
    for sign, out, near_x, far_x in ((1, to_left, 2, 3), (-1, to_right, 9, 8)):
        near, far = face_rows(0, sign)
        for slot, i in enumerate(near):
            out[slot] = ext[i, near_x]
        for slot, i in enumerate(far):
            out[14 + slot] = ext[i, far_x]
        for axis in range(3):
            out[19 + axis] = vel[1, axis, near_x - 2]
        out[22] = (solid[near_x - 2] > 0).astype(F32)


def y_faces(ext_in, from_left, from_right, vel, solid, ext, to_down, to_up):
    del ext_in
    gx = lax.axis_index("gx")
    inner = gx > 0, gx < lax.axis_size("gx") - 1
    for sign, ref, ok, near_x, far_x in ((-1, from_left, inner[0], 1, 0), (1, from_right, inner[1], 10, 11)):
        near, far = face_rows(0, sign)
        for slot, i in enumerate(near):
            ext[i, near_x] = jnp.where(ok, ref[slot], 0.0)
        for slot, i in enumerate(far):
            ext[i, far_x] = jnp.where(ok, ref[14 + slot], 0.0)
    for sign, out, near_y, far_y in ((1, to_down, 0, 1), (-1, to_up, BY - 1, BY - 2)):
        near, far = face_rows(1, sign)
        out[...] = jnp.zeros((23, 16, BZ), F32)
        for base, pops, y in ((0, near, near_y), (14, far, far_y)):
            for slot, i in enumerate(pops):
                for x in range(EX):
                    if needed(i, x):
                        out[base + slot, x : x + 1, :] = ext[i, x, y : y + 1, :]
        for axis in range(3):
            out[19 + axis, 1:2, :] = from_left[19 + axis, near_y : near_y + 1, :]
            out[19 + axis, 10:11, :] = from_right[19 + axis, near_y : near_y + 1, :]
            for x in range(BX):
                out[19 + axis, x + 2 : x + 3, :] = vel[1, axis, x, near_y : near_y + 1, :]
        out[22, 1:2, :] = from_left[22, near_y : near_y + 1, :]
        out[22, 10:11, :] = from_right[22, near_y : near_y + 1, :]
        for x in range(BX):
            out[22, x + 2 : x + 3, :] = (solid[x, near_y : near_y + 1, :] > 0).astype(F32)


def needed(i, x):
    if x == 0:
        return VEL[i][0] == -1
    if x == 1:
        return VEL[i][0] in (0, -1)
    if x == EX - 2:
        return VEL[i][0] in (0, 1)
    if x == EX - 1:
        return VEL[i][0] == 1
    return True


def adjoint_collide(u, is_solid, r, want):
    square = u[0] * u[0] + u[1] * u[1] + u[2] * u[2]
    axis_sum = diag_sum = axis_quad = diag_quad = None
    axis_mom = [None, None, None]
    diag_mom = [None, None, None]

    def plus(a, b):
        return b if a is None else a + b

    for n, (ip, im, c) in enumerate(PAIRS):
        s, d = r[ip] + r[im], r[ip] - r[im]
        p = None
        for axis in range(3):
            if c[axis]:
                p = u[axis] if p is None else (p + u[axis] if c[axis] > 0 else p - u[axis])
        q = p * s
        m = d + 3.0 * q
        if n < 3:
            axis_sum, axis_quad = plus(axis_sum, s), plus(axis_quad, q * p)
            axis_mom[n] = m
        else:
            diag_sum, diag_quad = plus(diag_sum, s), plus(diag_quad, q * p)
            for axis in range(3):
                if c[axis] > 0:
                    diag_mom[axis] = plus(diag_mom[axis], m)
                elif c[axis] < 0:
                    diag_mom[axis] = diag_mom[axis] - m
    scale = 1.0 / RELAX
    keep = 1.0 - scale
    total = (scale / 3.0) * r[0] + (scale / 18.0) * axis_sum + (scale / 36.0) * diag_sum
    quad = (4.5 * scale / 18.0) * axis_quad + (4.5 * scale / 36.0) * diag_quad
    density = total * (1.0 + 1.5 * square) - quad
    triple = 3.0 * total
    grad = [
        (3.0 * scale / 18.0) * axis_mom[a] + (3.0 * scale / 36.0) * diag_mom[a] - triple * u[a] for a in range(3)
    ]
    out = {}
    if 0 in want:
        out[0] = jnp.where(is_solid, r[0], keep * r[0] + density)
    for ip, im, c in PAIRS:
        if ip not in want and im not in want:
            continue
        g = None
        for axis in range(3):
            if c[axis]:
                g = grad[axis] if g is None else (g + grad[axis] if c[axis] > 0 else g - grad[axis])
        if ip in want:
            out[ip] = jnp.where(is_solid, r[im], keep * r[ip] + (density + g))
        if im in want:
            out[im] = jnp.where(is_solid, r[ip], keep * r[im] + (density - g))
    return out


def shift_z(v, step):
    if step == 0:
        return v
    lane = iota(v.shape, 1)
    if step > 0:
        return jnp.where(lane == BZ - 1, 0.0, pltpu.roll(v, BZ - 1, 1))
    return jnp.where(lane == 0, 0.0, pltpu.roll(v, 1, 1))


NEAR_DOWN = {i: n for n, i in enumerate(face_rows(1, -1)[0])}
NEAR_UP = {i: n for n, i in enumerate(face_rows(1, 1)[0])}
FAR_DOWN = {i: n for n, i in enumerate(face_rows(1, -1)[1])}
FAR_UP = {i: n for n, i in enumerate(face_rows(1, 1)[1])}
ALL = list(range(19))


def read_plane(field, low_face, high_face, x, i, low_slot, high_slot):
    cx, cy, cz = VEL[i]
    v = field[i, x + cx]
    if cy:
        row = iota(v.shape, 0)
        if cy > 0:
            edge = high_face[high_slot[i], pl.ds(x + cx, 1), :]
            v = jnp.where(row == BY - 1, jnp.broadcast_to(edge, v.shape), pltpu.roll(v, BY - 1, 0))
        else:
            edge = low_face[low_slot[i], pl.ds(x + cx, 1), :]
            v = jnp.where(row == 0, jnp.broadcast_to(edge, v.shape), pltpu.roll(v, 1, 0))
    return shift_z(v, cz)


def collide_block(reads, load_u, load_solid, want, store):
    for h in range(2):
        for b in range(2):
            rows, lanes = slice(8 * h, 8 * h + 8), slice(128 * b, 128 * b + 128)
            r = [reads[i, rows, lanes] for i in range(19)]
            u = [load_u(axis, rows, lanes) for axis in range(3)]
            out = adjoint_collide(u, load_solid(rows, lanes), r, want)
            for i in want:
                store(i, rows, lanes, out[i])


def two_steps(
    ext, from_left, from_right, from_down, from_up, to_down, to_up, vel, solid,
    initial, middle, mid_ext, first, low_near, high_near, low_face, high_face, reads, mid_sems, first_sems,
):
    gx, gy = lax.axis_index("gx"), lax.axis_index("gy")
    in_left, in_right = gx > 0, gx < lax.axis_size("gx") - 1
    in_down, in_up = gy > 0, gy < lax.axis_size("gy") - 1
    for n in range(14):
        low_near[n] = jnp.where(in_down, from_down[n], 0.0)
        high_near[n] = jnp.where(in_up, from_up[n], 0.0)

    for x, ref, ok, sign in ((1, from_left, in_left, -1), (EX - 2, from_right, in_right, 1)):
        for i in range(19):
            reads[i] = read_plane(ext, low_near, high_near, x, i, NEAR_DOWN, NEAR_UP)

        def keep(i, rows, lanes, value, x=x, ok=ok):
            mid_ext[i, x, rows, lanes] = jnp.where(ok, value, 0.0)

        collide_block(
            reads,
            lambda axis, rows, lanes, ref=ref: ref[19 + axis, rows, lanes],
            lambda rows, lanes, ref=ref: ref[22, rows, lanes] > 0.0,
            face_rows(0, sign)[1],
            keep,
        )

    for ref, mine, near, far, sign, ok, out in (
        (from_down, to_down, NEAR_DOWN, FAR_DOWN, -1, in_down, low_face),
        (from_up, to_up, NEAR_UP, FAR_UP, 1, in_up, high_face),
    ):
        mine_near = NEAR_UP if sign < 0 else NEAR_DOWN
        for i in range(19):
            cx, cy, cz = VEL[i]
            if cy == 0:
                v = ref[near[i]]
            elif cy == sign:
                v = ref[14 + far[i]]
            else:
                v = mine[mine_near[i]]
            if cx:
                v = pltpu.roll(v, (-cx) % 16, 0)
            reads[i] = shift_z(v, cz)
        row = iota((8, 128), 0)

        def keep_row(i, rows, lanes, value, out=out, far=far, ok=ok):
            x = row + rows.start
            good = ok & ((x > 1) | in_left) & ((x < EX - 2) | in_right)
            out[far[i], rows, lanes] = jnp.where(good, value, 0.0)

        collide_block(
            reads,
            lambda axis, rows, lanes, ref=ref: ref[19 + axis, rows, lanes],
            lambda rows, lanes, ref=ref: ref[22, rows, lanes] > 0.0,
            face_rows(1, sign)[1],
            keep_row,
        )

    def mid_copy(x):
        return pltpu.make_async_copy(mid_ext.at[:, pl.ds(x + 2, 1)], middle.at[:, pl.ds(x, 1)], mid_sems.at[x])

    def first_copy(x):
        return pltpu.make_async_copy(first.at[:, pl.ds(x, 1)], initial.at[:, pl.ds(x, 1)], first_sems.at[x])

    def mid_plane(x, carry):
        for i in range(19):
            reads[i] = read_plane(ext, low_near, high_near, x + 2, i, NEAR_DOWN, NEAR_UP)

        def keep(i, rows, lanes, value):
            mid_ext[i, x + 2, rows, lanes] = value

        collide_block(
            reads,
            lambda axis, rows, lanes: vel[1, axis, x, rows, lanes],
            lambda rows, lanes: solid[x, rows, lanes] > 0,
            ALL,
            keep,
        )
        mid_copy(x).start()
        return carry

    lax.fori_loop(0, BX, mid_plane, 0)

    def first_plane(x, carry):
        for i in range(19):
            reads[i] = read_plane(mid_ext, low_face, high_face, x + 2, i, FAR_DOWN, FAR_UP)

        def keep(i, rows, lanes, value):
            first[i, x, rows, lanes] = value

        collide_block(
            reads,
            lambda axis, rows, lanes: vel[0, axis, x, rows, lanes],
            lambda rows, lanes: solid[x, rows, lanes] > 0,
            ALL,
            keep,
        )
        first_copy(x).start()
        return carry

    lax.fori_loop(0, BX, first_plane, 0)

    def finish(x, carry):
        mid_copy(x).wait()
        first_copy(x).wait()
        return carry

    lax.fori_loop(0, BX, finish, 0)


def shifted(value, axis, step):
    count = lax.axis_size(axis)
    return lax.ppermute(value, axis, [(i, (i + step) % count) for i in range(count)])


def body(adj_later, saved_pops, saved_scale, solid, seed_values, seed_contact, seed_cell):
    block = pltpu.VMEM((24, 128), F32)
    low, mid, high = call(
        group_items,
        (block,) * 3,
        [vmem] * 3,
        (seed_values.T, seed_contact.reshape(1, 128), seed_cell.reshape(1, 128)),
        scratch=[pltpu.VMEM((24, 128), F32)],
    )
    left = shifted(high, "gx", 1)
    right = shifted(low, "gx", -1)

    scale = saved_scale.transpose(0, 2, 3, 4, 1).reshape(2, BX, 2 * BY, 19)
    vel, ext = call(
        velocities,
        (pltpu.VMEM((2, 3, BX, BY, BZ), F32), pltpu.VMEM((19, EX, BY, BZ), F32)),
        [anyspace, vmem, anyspace],
        (saved_pops, scale, adj_later),
        scratch=[
            pltpu.VMEM((2, 19, BX, BY, BZ), jnp.bfloat16),
            pltpu.SemaphoreType.DMA((4,)),
            pltpu.SemaphoreType.DMA(()),
        ],
    )

    down, same, up = call(regroup, (block,) * 3, [vmem] * 3, (in_vmem(left), mid, in_vmem(right)))
    from_low = shifted(up, "gy", 1)
    from_high = shifted(down, "gy", -1)

    solid_v = in_vmem(solid)
    face = pltpu.VMEM((23, BY, BZ), F32)
    ext, to_left, to_right = call(
        scatter,
        (pltpu.VMEM((19, EX, BY, BZ), F32), face, face),
        [vmem] * 6,
        (ext, vel, solid_v, in_vmem(from_low), same, in_vmem(from_high)),
        scratch=[pltpu.VMEM((128, 384), jnp.bfloat16), pltpu.VMEM((768, BZ), jnp.bfloat16)],
        aliases={0: 0},
    )
    from_left = in_vmem(shifted(to_right, "gx", 1))
    from_right = in_vmem(shifted(to_left, "gx", -1))
    row_face = pltpu.VMEM((23, 16, BZ), F32)
    ext, to_down, to_up = call(
        y_faces,
        (pltpu.VMEM((19, EX, BY, BZ), F32), row_face, row_face),
        [vmem] * 5,
        (ext, from_left, from_right, vel, solid_v),
        aliases={0: 0},
    )
    from_down = in_vmem(shifted(to_up, "gy", 1))
    from_up = in_vmem(shifted(to_down, "gy", -1))
    field = jax.ShapeDtypeStruct((19, BX, BY, BZ), F32)
    return call(
        two_steps,
        (field, field),
        [vmem] * 9,
        (ext, from_left, from_right, from_down, from_up, to_down, to_up, vel, solid_v),
        scratch=[
            pltpu.VMEM((19, EX, BY, BZ), F32),
            pltpu.VMEM((19, BX, BY, BZ), F32),
            pltpu.VMEM((14, 16, BZ), F32),
            pltpu.VMEM((14, 16, BZ), F32),
            pltpu.VMEM((5, 16, BZ), F32),
            pltpu.VMEM((5, 16, BZ), F32),
            pltpu.VMEM((19, BY, BZ), F32),
            pltpu.SemaphoreType.DMA((BX,)),
            pltpu.SemaphoreType.DMA((BX,)),
        ],
    )


def solution(mesh):
    return jax.shard_map(
        body,
        mesh=mesh,
        in_specs=(
            P(None, "gx", "gy", None),
            P(None, None, "gx", "gy", None),
            P(None, None, "gx", "gy", None),
            P("gx", "gy", None),
            P(("gx", "gy"), None),
            P(("gx", "gy"), None),
            P(("gx", "gy")),
        ),
        out_specs=(P(None, "gx", "gy", None), P(None, "gx", "gy", None)),
        check_vma=False,
    )
```

```python
import functools

import jax
import jax.numpy as jnp
from jax import lax
from jax.experimental import pallas as pl
from jax.experimental.pallas import tpu as pltpu
from jax.sharding import PartitionSpec as P

PAIRS = [
    (1, 2, (1, 0, 0)),
    (3, 4, (0, 1, 0)),
    (5, 6, (0, 0, 1)),
    (7, 8, (1, 1, 0)),
    (9, 10, (1, -1, 0)),
    (11, 12, (1, 0, 1)),
    (13, 14, (1, 0, -1)),
    (15, 16, (0, 1, 1)),
    (17, 18, (0, 1, -1)),
]
VEL = [(0, 0, 0)] * 19
for _p, _m, _c in PAIRS:
    VEL[_p] = _c
    VEL[_m] = tuple(-v for v in _c)
OPP = [0] * 19
for _p, _m, _c in PAIRS:
    OPP[_p], OPP[_m] = _m, _p
RELAX = 0.8
F32 = jnp.float32
BX, BY, BZ = 8, 16, 256
EX = 12
LIST = 32


def face_rows(axis, sign):
    near = [i for i in range(19) if VEL[i][axis] in (0, sign)]
    far = [i for i in range(19) if VEL[i][axis] == sign]
    return near, far


vmem = pl.BlockSpec(memory_space=pltpu.VMEM)
anyspace = pl.BlockSpec(memory_space=pl.ANY)


hbm = pl.BlockSpec(memory_space=pltpu.HBM)


def in_vmem(x):
    return pltpu.with_memory_space_constraint(x, pltpu.VMEM)


def in_hbm(x):
    return pltpu.with_memory_space_constraint(x, pltpu.HBM)


def call(body, out_shape, in_specs, args, scratch=(), aliases=None, limit=20 << 20):
    single = not isinstance(out_shape, (tuple, list))
    outs = (out_shape,) if single else tuple(out_shape)
    out_specs = tuple(vmem if isinstance(o, type(pltpu.VMEM((8, 128), F32))) else anyspace for o in outs)
    res = pl.pallas_call(
        body,
        out_shape=outs,
        in_specs=in_specs,
        out_specs=out_specs,
        scratch_shapes=list(scratch),
        input_output_aliases=aliases or {},
        compiler_params=pltpu.CompilerParams(vmem_limit_bytes=limit),
    )(*args)
    return res[0] if single else res


def iota(shape, dim):
    return lax.broadcasted_iota(jnp.int32, shape, dim)


NEAR_DOWN = {i: n for n, i in enumerate(face_rows(1, -1)[0])}
NEAR_UP = {i: n for n, i in enumerate(face_rows(1, 1)[0])}
FAR_DOWN = {i: n for n, i in enumerate(face_rows(1, -1)[1])}
FAR_UP = {i: n for n, i in enumerate(face_rows(1, 1)[1])}
ALL = list(range(19))


def plane_velocity(pop, store):
    density = pop(0)
    mom = [None, None, None]
    for plus, minus, c in PAIRS:
        fp, fm = pop(plus), pop(minus)
        density = density + (fp + fm)
        d = fp - fm
        for axis in range(3):
            if c[axis]:
                if mom[axis] is None:
                    mom[axis] = d
                elif c[axis] > 0:
                    mom[axis] = mom[axis] + d
                else:
                    mom[axis] = mom[axis] - d
    inv = 1.0 / density
    for axis in range(3):
        store(axis, mom[axis] * inv)


def group_items(values, contact, cell, low, mid, high, pay, own_values, own_contact, own_cell, sems):
    copies = [
        pltpu.make_async_copy(src, dst, sems.at[n])
        for n, (src, dst) in enumerate(((contact, own_contact), (cell, own_cell), (values, own_values)))
    ]
    for c in copies:
        c.start()
    for c in copies:
        c.wait()
    code = own_contact[...]
    hot = (iota((16, 128), 0) == code).astype(jnp.bfloat16)
    before = (iota((128, 128), 0) < iota((128, 128), 1)).astype(jnp.bfloat16)
    counts = jnp.dot(hot, before, preferred_element_type=F32)
    rank = jnp.sum(jnp.where(iota((16, 128), 0) == code, counts, 0.0), axis=0, keepdims=True).astype(jnp.int32)
    third = (code >= 3).astype(jnp.int32) + (code >= 6).astype(jnp.int32)
    slot = third * 128 + (code - 3 * third) * LIST + rank
    pay[...] = jnp.zeros((24, 128), F32)
    pay[0:19, :] = own_values[...]
    pay[19:20, :] = own_cell[...].astype(F32)
    payload = pay[...]
    for part, out in enumerate((low, mid, high)):
        pick = (iota((128, 128), 0) + 128 * part == slot).astype(F32)
        out[...] = lax.dot_general(
            payload, pick, (((1,), (1,)), ((), ())), precision=lax.Precision.HIGHEST, preferred_element_type=F32
        )


def velocity_planes(pops, scale, step, vel, raw, table_all, sems):
    scale_copy = pltpu.make_async_copy(scale.at[step], table_all, sems.at[0])
    scale_copy.start()
    copies = []
    for h in range(2):
        c = pltpu.make_async_copy(pops.at[step, :, pl.ds(4 * h, 4)], raw.at[:, pl.ds(4 * h, 4)], sems.at[1 + h])
        c.start()
        copies.append(c)
    yield
    scale_copy.wait()
    for h, c in enumerate(copies):
        c.wait()

        def plane(x, carry):
            for b in range(2):
                lanes = slice(128 * b, 128 * b + 128)
                table = table_all[x, pl.ds(b, BY, stride=2), :]

                def pop(i):
                    return raw[i, x, :, lanes].astype(F32) * jnp.broadcast_to(table[:, i : i + 1], (BY, 128))

                def store(axis, value):
                    vel[axis, x, :, lanes] = value

                plane_velocity(pop, store)
            return carry

        lax.fori_loop(4 * h, 4 * h + 4, plane, 0)
    yield


def late_velocities(pops, scale, adj, solid_in, vel, ext, solid, raw, table_all, sems):
    work = velocity_planes(pops, scale, 1, vel, raw, table_all, sems)
    next(work)
    adj_copy = pltpu.make_async_copy(adj, ext.at[:, pl.ds(2, BX)], sems.at[3])
    adj_copy.start()
    solid_copy = pltpu.make_async_copy(solid_in, solid, sems.at[4])
    solid_copy.start()
    next(work)
    adj_copy.wait()
    solid_copy.wait()


def early_velocities(pops, scale, after, vel, raw, table_all, sems):
    del after
    work = velocity_planes(pops, scale, 0, vel, raw, table_all, sems)
    next(work)
    next(work)


def held(i, x):
    if x in (0, EX - 1):
        return VEL[i][0] == (-1 if x == 0 else 1)
    if x in (1, EX - 2):
        return VEL[i][0] in (0, -1 if x == 1 else 1)
    return True


def regroup(left, own, right, after, down, same, up):
    del after
    gx = lax.axis_index("gx")
    a = jnp.where(gx > 0, left[...], 0.0)
    b = own[...]
    c = jnp.where(gx < lax.axis_size("gx") - 1, right[...], 0.0)
    lane = iota((24, 128), 1)
    for j, out in enumerate((down, same, up)):
        ra = pltpu.roll(a, (-LIST * j) % 128, 1)
        rb = pltpu.roll(b, (LIST - LIST * j) % 128, 1)
        rc = pltpu.roll(c, (2 * LIST - LIST * j) % 128, 1)
        out[...] = jnp.where(
            lane < LIST, ra, jnp.where(lane < 2 * LIST, rb, jnp.where(lane < 3 * LIST, rc, 0.0))
        )


Y_ROWS = 23 * EX + 4


def put(entry, x):
    return slice(EX * entry + x, EX * entry + x + 1)


def y_faces(ext_in, from_left, from_right, vel, solid, ext, to_down, to_up):
    del ext_in
    gx = lax.axis_index("gx")
    in_left, in_right = gx > 0, gx < lax.axis_size("gx") - 1
    for sign, ref, ok, near_x, far_x in ((-1, from_left, in_left, 1, 0), (1, from_right, in_right, 10, 11)):
        near, far = face_rows(0, sign)
        for slot, i in enumerate(near):
            ext[i, near_x] = jnp.where(ok, ref[slot], 0.0)
        for slot, i in enumerate(far):
            ext[i, far_x] = jnp.where(ok, ref[14 + slot], 0.0)
    for sign, out, near_y, far_y in ((1, to_down, 0, 1), (-1, to_up, BY - 1, BY - 2)):
        near, far = face_rows(1, sign)
        out[...] = jnp.zeros((Y_ROWS, BZ), F32)
        for base, pops, y in ((0, near, near_y), (14, far, far_y)):
            for slot, i in enumerate(pops):
                for x in range(EX):
                    if held(i, x):
                        out[put(base + slot, x), :] = ext[i, x, y : y + 1, :]
        for row in range(19, 23):
            out[put(row, 1), :] = from_left[row, near_y : near_y + 1, :]
            out[put(row, 10), :] = from_right[row, near_y : near_y + 1, :]
        for x in range(BX):
            for axis in range(3):
                out[put(19 + axis, x + 2), :] = vel[axis, x, near_y : near_y + 1, :]
            out[put(22, x + 2), :] = (solid[x, near_y : near_y + 1, :] > 0).astype(F32)


def halves(v):
    hi = v.astype(jnp.bfloat16)
    return hi, (v - hi.astype(F32)).astype(jnp.bfloat16)


def one_hot(rows, targets):
    return (iota((rows, targets.shape[1]), 0) == targets).astype(F32).astype(jnp.bfloat16)


def contract_lanes(a, b):
    return lax.dot_general(a, b, (((1,), (1,)), ((), ())), preferred_element_type=F32)


def scatter(ext_in, down, same, up, vel, solid, ext, to_left, to_right, merged, where_xy, where_z):
    del ext_in
    gy = lax.axis_index("gy")
    merged[:, 0:128] = jnp.where(gy > 0, down[...], 0.0)
    merged[:, 128:256] = same[...]
    merged[:, 256:384] = jnp.where(gy < lax.axis_size("gy") - 1, up[...], 0.0)
    cell = merged[19:20, :].astype(jnp.int32)
    where_xy[...] = one_hot(128, cell // BZ)
    where_z[...] = one_hot(BZ, cell % BZ)
    for i in range(19):
        hi, lo = halves(merged[i : i + 1, :])
        rows = where_xy[...]
        field = contract_lanes(jnp.concatenate([rows * hi, rows * lo], axis=0), where_z[...])
        ext[i, 2 : 2 + BX] = ext[i, 2 : 2 + BX] + (field[0:128] + field[128:256]).reshape(BX, BY, BZ)
    for sign, out, near_x, far_x in ((1, to_left, 2, 3), (-1, to_right, 9, 8)):
        near, far = face_rows(0, sign)
        for slot, i in enumerate(near):
            out[slot] = ext[i, near_x]
        for slot, i in enumerate(far):
            out[14 + slot] = ext[i, far_x]
        for axis in range(3):
            out[19 + axis] = vel[axis, near_x - 2]
        out[22] = (solid[near_x - 2] > 0).astype(F32)


def adjoint_collide(u, is_solid, r, want):
    square = u[0] * u[0] + u[1] * u[1] + u[2] * u[2]
    axis_sum = diag_sum = axis_quad = diag_quad = None
    axis_mom = [None, None, None]
    diag_mom = [None, None, None]

    def plus(a, b):
        return b if a is None else a + b

    for n, (ip, im, c) in enumerate(PAIRS):
        s, d = r[ip] + r[im], r[ip] - r[im]
        p = None
        for axis in range(3):
            if c[axis]:
                p = u[axis] if p is None else (p + u[axis] if c[axis] > 0 else p - u[axis])
        q = p * s
        m = d + 3.0 * q
        if n < 3:
            axis_sum, axis_quad = plus(axis_sum, s), plus(axis_quad, q * p)
            axis_mom[n] = m
        else:
            diag_sum, diag_quad = plus(diag_sum, s), plus(diag_quad, q * p)
            for axis in range(3):
                if c[axis] > 0:
                    diag_mom[axis] = plus(diag_mom[axis], m)
                elif c[axis] < 0:
                    diag_mom[axis] = diag_mom[axis] - m
    scale = 1.0 / RELAX
    keep = 1.0 - scale
    total = (scale / 3.0) * r[0] + (scale / 18.0) * axis_sum + (scale / 36.0) * diag_sum
    quad = (4.5 * scale / 18.0) * axis_quad + (4.5 * scale / 36.0) * diag_quad
    density = total * (1.0 + 1.5 * square) - quad
    triple = 3.0 * total
    grad = [
        (3.0 * scale / 18.0) * axis_mom[a] + (3.0 * scale / 36.0) * diag_mom[a] - triple * u[a] for a in range(3)
    ]
    out = {}
    if 0 in want:
        out[0] = jnp.where(is_solid, r[0], keep * r[0] + density)
    for ip, im, c in PAIRS:
        if ip not in want and im not in want:
            continue
        g = None
        for axis in range(3):
            if c[axis]:
                g = grad[axis] if g is None else (g + grad[axis] if c[axis] > 0 else g - grad[axis])
        if ip in want:
            out[ip] = jnp.where(is_solid, r[im], keep * r[ip] + (density + g))
        if im in want:
            out[im] = jnp.where(is_solid, r[ip], keep * r[im] + (density - g))
    return out


def shift_z(v, step):
    if step == 0:
        return v
    lane = iota(v.shape, 1)
    if step > 0:
        return jnp.where(lane == BZ - 1, 0.0, pltpu.roll(v, BZ - 1, 1))
    return jnp.where(lane == 0, 0.0, pltpu.roll(v, 1, 1))


def read_plane(field, low_face, high_face, x, i, low_slot, high_slot):
    cx, cy, cz = VEL[i]
    v = field[i, x + cx]
    if cy:
        row = iota(v.shape, 0)
        if cy > 0:
            edge = high_face[high_slot[i], pl.ds(x + cx, 1), :]
            v = jnp.where(row == BY - 1, jnp.broadcast_to(edge, v.shape), pltpu.roll(v, BY - 1, 0))
        else:
            edge = low_face[low_slot[i], pl.ds(x + cx, 1), :]
            v = jnp.where(row == 0, jnp.broadcast_to(edge, v.shape), pltpu.roll(v, 1, 0))
    return shift_z(v, cz)


def collide_block(reads, load_u, load_solid, want, store):
    for h in range(2):
        for b in range(2):
            rows, lanes = slice(8 * h, 8 * h + 8), slice(128 * b, 128 * b + 128)
            r = [reads[i, rows, lanes] for i in range(19)]
            u = [load_u(axis, rows, lanes) for axis in range(3)]
            out = adjoint_collide(u, load_solid(rows, lanes), r, want)
            for i in want:
                store(i, rows, lanes, out[i])


def entry(face, n):
    return face[EX * n : EX * n + 16, :]


def two_steps(
    ext, from_left, from_right, from_down, from_up, to_down, to_up, vel_late, vel_early, solid,
    initial, middle,
    mid_ext, first, low_near, high_near, low_face, high_face, reads, mid_sems, first_sems,
):
    gx, gy = lax.axis_index("gx"), lax.axis_index("gy")
    in_left, in_right = gx > 0, gx < lax.axis_size("gx") - 1
    in_down, in_up = gy > 0, gy < lax.axis_size("gy") - 1

    for n in range(14):
        low_near[n] = jnp.where(in_down, entry(from_down, n), 0.0)
        high_near[n] = jnp.where(in_up, entry(from_up, n), 0.0)

    for x, ref, ok, sign in ((1, from_left, in_left, -1), (EX - 2, from_right, in_right, 1)):
        for i in range(19):
            reads[i] = read_plane(ext, low_near, high_near, x, i, NEAR_DOWN, NEAR_UP)

        def keep(i, rows, lanes, value, x=x, ok=ok):
            mid_ext[i, x, rows, lanes] = jnp.where(ok, value, 0.0)

        collide_block(
            reads,
            lambda axis, rows, lanes, ref=ref: ref[19 + axis, rows, lanes],
            lambda rows, lanes, ref=ref: ref[22, rows, lanes] > 0.0,
            face_rows(0, sign)[1],
            keep,
        )

    for ref, mine, mine_slot, near, far, sign, ok, out in (
        (from_down, to_down, NEAR_UP, NEAR_DOWN, FAR_DOWN, -1, in_down, low_face),
        (from_up, to_up, NEAR_DOWN, NEAR_UP, FAR_UP, 1, in_up, high_face),
    ):
        for i in range(19):
            cx, cy, cz = VEL[i]
            if cy == 0:
                v = entry(ref, near[i])
            elif cy == sign:
                v = entry(ref, 14 + far[i])
            else:
                v = entry(mine, mine_slot[i])
            if cx:
                v = pltpu.roll(v, (-cx) % 16, 0)
            reads[i] = shift_z(v, cz)
        row = iota((8, 128), 0)

        def keep_row(i, rows, lanes, value, out=out, far=far, ok=ok):
            x = row + rows.start
            good = ok & ((x > 1) | in_left) & ((x < EX - 2) | in_right)
            out[far[i], rows, lanes] = jnp.where(good, value, 0.0)

        collide_block(
            reads,
            lambda axis, rows, lanes, ref=ref: entry(ref, 19 + axis)[rows, lanes],
            lambda rows, lanes, ref=ref: entry(ref, 22)[rows, lanes] > 0.0,
            face_rows(1, sign)[1],
            keep_row,
        )

    def mid_copy(x):
        return pltpu.make_async_copy(mid_ext.at[:, pl.ds(x + 2, 1)], middle.at[:, pl.ds(x, 1)], mid_sems.at[x])

    def first_copy(x):
        return pltpu.make_async_copy(first.at[:, pl.ds(x, 1)], initial.at[:, pl.ds(x, 1)], first_sems.at[x])

    def mid_plane(x, carry):
        for i in range(19):
            reads[i] = read_plane(ext, low_near, high_near, x + 2, i, NEAR_DOWN, NEAR_UP)

        def keep(i, rows, lanes, value):
            mid_ext[i, x + 2, rows, lanes] = value

        collide_block(
            reads,
            lambda axis, rows, lanes: vel_late[axis, x, rows, lanes],
            lambda rows, lanes: solid[x, rows, lanes] > 0,
            ALL,
            keep,
        )
        mid_copy(x).start()
        return carry

    lax.fori_loop(0, BX, mid_plane, 0)

    def first_plane(x, carry):
        for i in range(19):
            reads[i] = read_plane(mid_ext, low_face, high_face, x + 2, i, FAR_DOWN, FAR_UP)

        def keep(i, rows, lanes, value):
            first[i, x, rows, lanes] = value

        collide_block(
            reads,
            lambda axis, rows, lanes: vel_early[axis, x, rows, lanes],
            lambda rows, lanes: solid[x, rows, lanes] > 0,
            ALL,
            keep,
        )
        first_copy(x).start()
        return carry

    lax.fori_loop(0, BX, first_plane, 0)

    def finish(x, carry):
        mid_copy(x).wait()
        first_copy(x).wait()
        return carry

    lax.fori_loop(0, BX, finish, 0)


def shifted(value, axis, step):
    count = lax.axis_size(axis)
    return lax.ppermute(value, axis, [(i, (i + step) % count) for i in range(count)])


def body(adj_later, saved_pops, saved_scale, solid, seed_values, seed_contact, seed_cell):
    adj, pops, solid_h = in_hbm(adj_later), in_hbm(saved_pops), in_hbm(solid)
    scale = in_hbm(saved_scale.transpose(0, 2, 3, 4, 1).reshape(2, BX, 2 * BY, 19))
    block = pltpu.VMEM((24, 128), F32)
    x_face = pltpu.VMEM((23, BY, BZ), F32)
    y_face = pltpu.VMEM((Y_ROWS, BZ), F32)
    extended = pltpu.VMEM((19, EX, BY, BZ), F32)
    flow = pltpu.VMEM((3, BX, BY, BZ), F32)
    low, mid, high = call(
        group_items,
        (block,) * 3,
        [hbm] * 3,
        (in_hbm(seed_values.T), in_hbm(seed_contact.reshape(1, 128)), in_hbm(seed_cell.reshape(1, 128))),
        scratch=[
            pltpu.VMEM((24, 128), F32),
            pltpu.VMEM((19, 128), F32),
            pltpu.VMEM((1, 128), jnp.int32),
            pltpu.VMEM((1, 128), jnp.int32),
            pltpu.SemaphoreType.DMA((3,)),
        ],
    )
    left = in_vmem(shifted(high, "gx", 1))
    right = in_vmem(shifted(low, "gx", -1))

    raw = pltpu.VMEM((19, BX, BY, BZ), jnp.bfloat16)
    table = pltpu.VMEM((BX, 2 * BY, 19), F32)
    vel_late, ext, solid_v = call(
        late_velocities,
        (flow, extended, pltpu.VMEM((BX, BY, BZ), jnp.int32)),
        [hbm] * 4,
        (pops, scale, adj, solid_h),
        scratch=[raw, table, pltpu.SemaphoreType.DMA((5,))],
    )
    down, same, up = call(regroup, (block,) * 3, [vmem] * 4, (left, mid, right, solid_v))
    from_low = in_vmem(shifted(up, "gy", 1))
    from_high = in_vmem(shifted(down, "gy", -1))
    vel_early = call(
        early_velocities, flow, [hbm, hbm, vmem], (pops, scale, same),
        scratch=[raw, table, pltpu.SemaphoreType.DMA((3,))],
    )
    ext, to_left, to_right = call(
        scatter,
        (extended, x_face, x_face),
        [vmem] * 6,
        (ext, from_low, same, from_high, vel_late, solid_v),
        scratch=[
            pltpu.VMEM((24, 384), F32), pltpu.VMEM((128, 384), jnp.bfloat16), pltpu.VMEM((BZ, 384), jnp.bfloat16),
        ],
        aliases={0: 0},
    )
    from_left = in_vmem(shifted(to_right, "gx", 1))
    from_right = in_vmem(shifted(to_left, "gx", -1))
    ext, to_down, to_up = call(
        y_faces,
        (extended, y_face, y_face),
        [vmem] * 5,
        (ext, from_left, from_right, vel_late, solid_v),
        aliases={0: 0},
    )
    from_down = in_vmem(shifted(to_up, "gy", 1))
    from_up = in_vmem(shifted(to_down, "gy", -1))
    field = jax.ShapeDtypeStruct((19, BX, BY, BZ), F32)
    return call(
        two_steps,
        (field, field),
        [vmem] * 10,
        (ext, from_left, from_right, from_down, from_up, to_down, to_up, vel_late, vel_early, solid_v),
        scratch=[
            pltpu.VMEM((19, EX, BY, BZ), F32),
            pltpu.VMEM((19, BX, BY, BZ), F32),
            pltpu.VMEM((14, 16, BZ), F32),
            pltpu.VMEM((14, 16, BZ), F32),
            pltpu.VMEM((5, 16, BZ), F32),
            pltpu.VMEM((5, 16, BZ), F32),
            pltpu.VMEM((19, BY, BZ), F32),
            pltpu.SemaphoreType.DMA((BX,)),
            pltpu.SemaphoreType.DMA((BX,)),
        ],
    )


def solution(mesh):
    return jax.shard_map(
        body,
        mesh=mesh,
        in_specs=(
            P(None, "gx", "gy", None),
            P(None, None, "gx", "gy", None),
            P(None, None, "gx", "gy", None),
            P("gx", "gy", None),
            P(("gx", "gy"), None),
            P(("gx", "gy"), None),
            P(("gx", "gy")),
        ),
        out_specs=(P(None, "gx", "gy", None), P(None, "gx", "gy", None)),
        check_vma=False,
    )
```

```python
import functools

import jax
import jax.numpy as jnp
from jax import lax
from jax.experimental import pallas as pl
from jax.experimental.pallas import tpu as pltpu
from jax.sharding import PartitionSpec as P

PAIRS = [
    (1, 2, (1, 0, 0)),
    (3, 4, (0, 1, 0)),
    (5, 6, (0, 0, 1)),
    (7, 8, (1, 1, 0)),
    (9, 10, (1, -1, 0)),
    (11, 12, (1, 0, 1)),
    (13, 14, (1, 0, -1)),
    (15, 16, (0, 1, 1)),
    (17, 18, (0, 1, -1)),
]
VEL = [(0, 0, 0)] * 19
for _p, _m, _c in PAIRS:
    VEL[_p] = _c
    VEL[_m] = tuple(-v for v in _c)
OPP = [0] * 19
for _p, _m, _c in PAIRS:
    OPP[_p], OPP[_m] = _m, _p
RELAX = 0.8
F32 = jnp.float32
BX, BY, BZ = 8, 16, 256
EX = 12
LIST = 32


def face_rows(axis, sign):
    near = [i for i in range(19) if VEL[i][axis] in (0, sign)]
    far = [i for i in range(19) if VEL[i][axis] == sign]
    return near, far


vmem = pl.BlockSpec(memory_space=pltpu.VMEM)
anyspace = pl.BlockSpec(memory_space=pl.ANY)


hbm = pl.BlockSpec(memory_space=pltpu.HBM)


def in_vmem(x):
    return pltpu.with_memory_space_constraint(x, pltpu.VMEM)


def in_hbm(x):
    return pltpu.with_memory_space_constraint(x, pltpu.HBM)


def call(body, out_shape, in_specs, args, scratch=(), aliases=None, limit=20 << 20):
    single = not isinstance(out_shape, (tuple, list))
    outs = (out_shape,) if single else tuple(out_shape)
    out_specs = tuple(vmem if isinstance(o, type(pltpu.VMEM((8, 128), F32))) else anyspace for o in outs)
    res = pl.pallas_call(
        body,
        out_shape=outs,
        in_specs=in_specs,
        out_specs=out_specs,
        scratch_shapes=list(scratch),
        input_output_aliases=aliases or {},
        compiler_params=pltpu.CompilerParams(vmem_limit_bytes=limit),
    )(*args)
    return res[0] if single else res


def iota(shape, dim):
    return lax.broadcasted_iota(jnp.int32, shape, dim)


NEAR_DOWN = {i: n for n, i in enumerate(face_rows(1, -1)[0])}
NEAR_UP = {i: n for n, i in enumerate(face_rows(1, 1)[0])}
FAR_DOWN = {i: n for n, i in enumerate(face_rows(1, -1)[1])}
FAR_UP = {i: n for n, i in enumerate(face_rows(1, 1)[1])}
ALL = list(range(19))


def plane_velocity(pop, store):
    density = pop(0)
    mom = [None, None, None]
    for plus, minus, c in PAIRS:
        fp, fm = pop(plus), pop(minus)
        density = density + (fp + fm)
        d = fp - fm
        for axis in range(3):
            if c[axis]:
                if mom[axis] is None:
                    mom[axis] = d
                elif c[axis] > 0:
                    mom[axis] = mom[axis] + d
                else:
                    mom[axis] = mom[axis] - d
    inv = 1.0 / density
    for axis in range(3):
        store(axis, mom[axis] * inv)


def group_items(values, contact, cell, low, mid, high, pay, own_values, own_contact, own_cell, sems):
    copies = [
        pltpu.make_async_copy(src, dst, sems.at[n])
        for n, (src, dst) in enumerate(((contact, own_contact), (cell, own_cell), (values, own_values)))
    ]
    for c in copies:
        c.start()
    for c in copies:
        c.wait()
    code = own_contact[...]
    hot = (iota((16, 128), 0) == code).astype(jnp.bfloat16)
    before = (iota((128, 128), 0) < iota((128, 128), 1)).astype(jnp.bfloat16)
    counts = jnp.dot(hot, before, preferred_element_type=F32)
    rank = jnp.sum(jnp.where(iota((16, 128), 0) == code, counts, 0.0), axis=0, keepdims=True).astype(jnp.int32)
    third = (code >= 3).astype(jnp.int32) + (code >= 6).astype(jnp.int32)
    slot = (code - 3 * third) * 128 + third * LIST + rank
    pay[...] = jnp.zeros((24, 128), F32)
    pay[0:19, :] = own_values[...]
    pay[19:20, :] = own_cell[...].astype(F32)
    payload = pay[...]
    for part, out in enumerate((low, mid, high)):
        pick = (iota((128, 128), 0) + 128 * part == slot).astype(F32)
        out[...] = lax.dot_general(
            payload, pick, (((1,), (1,)), ((), ())), precision=lax.Precision.HIGHEST, preferred_element_type=F32
        )


def velocity_planes(pops, scale, step, vel, raw, table_all, sems):
    scale_copy = pltpu.make_async_copy(scale.at[step], table_all, sems.at[0])
    scale_copy.start()
    copies = []
    for h in range(2):
        c = pltpu.make_async_copy(pops.at[step, :, pl.ds(4 * h, 4)], raw.at[:, pl.ds(4 * h, 4)], sems.at[1 + h])
        c.start()
        copies.append(c)
    yield
    scale_copy.wait()
    for h, c in enumerate(copies):
        c.wait()

        def plane(x, carry):
            for b in range(2):
                lanes = slice(128 * b, 128 * b + 128)
                table = table_all[x, pl.ds(b, BY, stride=2), :]

                def pop(i):
                    return raw[i, x, :, lanes].astype(F32) * jnp.broadcast_to(table[:, i : i + 1], (BY, 128))

                def store(axis, value):
                    vel[axis, x, :, lanes] = value

                plane_velocity(pop, store)
            return carry

        lax.fori_loop(4 * h, 4 * h + 4, plane, 0)
    yield


def late_velocities(pops, scale, adj, solid_in, vel, ext, solid, raw, table_all, sems):
    work = velocity_planes(pops, scale, 1, vel, raw, table_all, sems)
    next(work)
    adj_copy = pltpu.make_async_copy(adj, ext.at[:, pl.ds(2, BX)], sems.at[3])
    adj_copy.start()
    solid_copy = pltpu.make_async_copy(solid_in, solid, sems.at[4])
    solid_copy.start()
    next(work)
    adj_copy.wait()
    solid_copy.wait()


def early_velocities(pops, scale, after, vel, raw, table_all, sems):
    del after
    work = velocity_planes(pops, scale, 0, vel, raw, table_all, sems)
    next(work)
    next(work)


def held(i, x):
    if x in (0, EX - 1):
        return VEL[i][0] == (-1 if x == 0 else 1)
    if x in (1, EX - 2):
        return VEL[i][0] in (0, -1 if x == 1 else 1)
    return True


def regroup(below, own, above, after, west, here, east):
    del after
    gy = lax.axis_index("gy")
    a = jnp.where(gy > 0, below[...], 0.0)
    b = own[...]
    c = jnp.where(gy < lax.axis_size("gy") - 1, above[...], 0.0)
    lane = iota((24, 128), 1)
    for j, out in enumerate((west, here, east)):
        ra = pltpu.roll(a, (-LIST * j) % 128, 1)
        rb = pltpu.roll(b, (LIST - LIST * j) % 128, 1)
        rc = pltpu.roll(c, (2 * LIST - LIST * j) % 128, 1)
        out[...] = jnp.where(
            lane < LIST, ra, jnp.where(lane < 2 * LIST, rb, jnp.where(lane < 3 * LIST, rc, 0.0))
        )


Y_ROWS = 23 * EX + 4


def put(entry, x):
    return slice(EX * entry + x, EX * entry + x + 1)


def halves(v):
    hi = v.astype(jnp.bfloat16)
    return hi, (v - hi.astype(F32)).astype(jnp.bfloat16)


def one_hot(rows, targets):
    return (iota((rows, targets.shape[1]), 0) == targets).astype(F32).astype(jnp.bfloat16)


def contract_lanes(a, b):
    return lax.dot_general(a, b, (((1,), (1,)), ((), ())), preferred_element_type=F32)


def add_own(ext, items, where_xy, where_z):
    cell = items[19:20, :].astype(jnp.int32)
    where_xy[...] = one_hot(128, cell // BZ)
    where_z[...] = one_hot(BZ, cell % BZ)
    for i in range(19):
        hi, lo = halves(items[i : i + 1, :])
        rows = where_xy[...]
        field = contract_lanes(jnp.concatenate([rows * hi, rows * lo], axis=0), where_z[...])
        ext[i, 2 : 2 + BX] = ext[i, 2 : 2 + BX] + (field[0:128] + field[128:256]).reshape(BX, BY, BZ)


def own_seeds(ext_in, west, here, east, vel, solid, ext, to_left, to_right, where_xy, where_z):
    del ext_in
    add_own(ext, here, where_xy, where_z)
    for sign, out, items, near_x, far_x in ((1, to_left, west, 2, 3), (-1, to_right, east, 9, 8)):
        near, far = face_rows(0, sign)
        for slot, i in enumerate(near):
            out[slot] = ext[i, near_x]
        for slot, i in enumerate(far):
            out[14 + slot] = ext[i, far_x]
        for axis in range(3):
            out[19 + axis] = vel[axis, near_x - 2]
        out[22] = (solid[near_x - 2] > 0).astype(F32)
        out[23, :, 0:128] = items[0:16, :]
        out[23, 0:8, 128:256] = items[16:24, :]
        out[23, 8:16, 128:256] = jnp.zeros((8, 128), F32)


def halo_scatter(items, near_rows, near_target, far_rows, far_target, height, add, stack):
    near_hot, far_hot = one_hot(16, near_target), one_hot(16, far_target)
    entries = [(near_hot, i, 0) for i in near_rows] + [(far_hot, i, 1) for i in far_rows]
    count = len(entries)
    for n, (hot, i, deep) in enumerate(entries):
        hi, lo = halves(items[i : i + 1, :])
        stack[16 * n : 16 * n + 16, :] = hot * hi
        stack[16 * (count + n) : 16 * (count + n) + 16, :] = hot * lo
    field = contract_lanes(stack[...], one_hot(BZ, height))
    for n, (hot, i, deep) in enumerate(entries):
        add(i, deep, field[16 * n : 16 * n + 16] + field[16 * (count + n) : 16 * (count + n) + 16])


def y_faces(
    ext_in, from_left, from_right, far_left, far_right, west, east, vel, solid,
    ext, to_down, to_up,
    items, where_xy, where_z, stack,
):
    del ext_in
    gx, last = lax.axis_index("gx"), lax.axis_size("gx") - 1
    for n, (face, ok) in enumerate(((from_left, gx > 0), (from_right, gx < last))):
        lanes = slice(128 * n, 128 * n + 128)
        items[0:16, lanes] = jnp.where(ok, face[23, :, 0:128], 0.0)
        items[16:24, lanes] = jnp.where(ok, face[23, 0:8, 128:256], 0.0)
    add_own(ext, items, where_xy, where_z)
    for sign, ref, mine, other, ok, other_ok, near_x, far_x, near_cell in (
        (-1, from_left, west, far_left, gx > 0, gx > 1, 1, 0, BX - 1),
        (1, from_right, east, far_right, gx < last, gx < last - 1, 10, 11, 0),
    ):
        near, far = face_rows(0, sign)
        slots = {i: n for n, i in enumerate(near)}, {i: 14 + n for n, i in enumerate(far)}
        items[:, 0:128] = mine[...]
        items[:, 128:256] = jnp.where(other_ok, other[...], 0.0)
        cell = items[19:20, :].astype(jnp.int32)
        x, y = cell // (BY * BZ), (cell // BZ) % BY

        def add(i, deep, field, ref=ref, ok=ok, near_x=near_x, far_x=far_x, slots=slots):
            ext[i, far_x if deep else near_x] = jnp.where(ok, ref[slots[deep][i]] + field, 0.0)

        halo_scatter(
            items, near, jnp.where(x == near_cell, y, -1), far, jnp.where(x == near_cell + sign, y, -1),
            cell % BZ, add, stack,
        )
    for sign, out, near_y, far_y in ((1, to_down, 0, 1), (-1, to_up, BY - 1, BY - 2)):
        near, far = face_rows(1, sign)
        out[...] = jnp.zeros((Y_ROWS, BZ), F32)
        for base, pops, y in ((0, near, near_y), (14, far, far_y)):
            for slot, i in enumerate(pops):
                for x in range(EX):
                    if held(i, x):
                        out[put(base + slot, x), :] = ext[i, x, y : y + 1, :]
        for row in range(19, 23):
            out[put(row, 1), :] = from_left[row, near_y : near_y + 1, :]
            out[put(row, 10), :] = from_right[row, near_y : near_y + 1, :]
        for x in range(BX):
            for axis in range(3):
                out[put(19 + axis, x + 2), :] = vel[axis, x, near_y : near_y + 1, :]
            out[put(22, x + 2), :] = (solid[x, near_y : near_y + 1, :] > 0).astype(F32)


def adjoint_collide(u, is_solid, r, want):
    square = u[0] * u[0] + u[1] * u[1] + u[2] * u[2]
    axis_sum = diag_sum = axis_quad = diag_quad = None
    axis_mom = [None, None, None]
    diag_mom = [None, None, None]

    def plus(a, b):
        return b if a is None else a + b

    for n, (ip, im, c) in enumerate(PAIRS):
        s, d = r[ip] + r[im], r[ip] - r[im]
        p = None
        for axis in range(3):
            if c[axis]:
                p = u[axis] if p is None else (p + u[axis] if c[axis] > 0 else p - u[axis])
        q = p * s
        m = d + 3.0 * q
        if n < 3:
            axis_sum, axis_quad = plus(axis_sum, s), plus(axis_quad, q * p)
            axis_mom[n] = m
        else:
            diag_sum, diag_quad = plus(diag_sum, s), plus(diag_quad, q * p)
            for axis in range(3):
                if c[axis] > 0:
                    diag_mom[axis] = plus(diag_mom[axis], m)
                elif c[axis] < 0:
                    diag_mom[axis] = diag_mom[axis] - m
    scale = 1.0 / RELAX
    keep = 1.0 - scale
    total = (scale / 3.0) * r[0] + (scale / 18.0) * axis_sum + (scale / 36.0) * diag_sum
    quad = (4.5 * scale / 18.0) * axis_quad + (4.5 * scale / 36.0) * diag_quad
    density = total * (1.0 + 1.5 * square) - quad
    triple = 3.0 * total
    grad = [
        (3.0 * scale / 18.0) * axis_mom[a] + (3.0 * scale / 36.0) * diag_mom[a] - triple * u[a] for a in range(3)
    ]
    out = {}
    if 0 in want:
        out[0] = jnp.where(is_solid, r[0], keep * r[0] + density)
    for ip, im, c in PAIRS:
        if ip not in want and im not in want:
            continue
        g = None
        for axis in range(3):
            if c[axis]:
                g = grad[axis] if g is None else (g + grad[axis] if c[axis] > 0 else g - grad[axis])
        if ip in want:
            out[ip] = jnp.where(is_solid, r[im], keep * r[ip] + (density + g))
        if im in want:
            out[im] = jnp.where(is_solid, r[ip], keep * r[im] + (density - g))
    return out


def shift_z(v, step):
    if step == 0:
        return v
    lane = iota(v.shape, 1)
    if step > 0:
        return jnp.where(lane == BZ - 1, 0.0, pltpu.roll(v, BZ - 1, 1))
    return jnp.where(lane == 0, 0.0, pltpu.roll(v, 1, 1))


def read_plane(field, low_face, high_face, x, i, low_slot, high_slot):
    cx, cy, cz = VEL[i]
    v = field[i, x + cx]
    if cy:
        row = iota(v.shape, 0)
        if cy > 0:
            edge = high_face[high_slot[i], pl.ds(x + cx, 1), :]
            v = jnp.where(row == BY - 1, jnp.broadcast_to(edge, v.shape), pltpu.roll(v, BY - 1, 0))
        else:
            edge = low_face[low_slot[i], pl.ds(x + cx, 1), :]
            v = jnp.where(row == 0, jnp.broadcast_to(edge, v.shape), pltpu.roll(v, 1, 0))
    return shift_z(v, cz)


def collide_block(reads, load_u, load_solid, want, store):
    for h in range(2):
        for b in range(2):
            rows, lanes = slice(8 * h, 8 * h + 8), slice(128 * b, 128 * b + 128)
            r = [reads[i, rows, lanes] for i in range(19)]
            u = [load_u(axis, rows, lanes) for axis in range(3)]
            out = adjoint_collide(u, load_solid(rows, lanes), r, want)
            for i in want:
                store(i, rows, lanes, out[i])


def entry(face, n):
    return face[EX * n : EX * n + 16, :]


def two_steps(
    ext, from_left, from_right, from_down, from_up, to_down, to_up, vel_late, vel_early, solid,
    initial, middle,
    mid_ext, first, low_near, high_near, low_face, high_face, reads, mid_sems, first_sems,
):
    gx, gy = lax.axis_index("gx"), lax.axis_index("gy")
    in_left, in_right = gx > 0, gx < lax.axis_size("gx") - 1
    in_down, in_up = gy > 0, gy < lax.axis_size("gy") - 1

    for n in range(14):
        low_near[n] = jnp.where(in_down, entry(from_down, n), 0.0)
        high_near[n] = jnp.where(in_up, entry(from_up, n), 0.0)

    for x, ref, ok, sign in ((1, from_left, in_left, -1), (EX - 2, from_right, in_right, 1)):
        for i in range(19):
            reads[i] = read_plane(ext, low_near, high_near, x, i, NEAR_DOWN, NEAR_UP)

        def keep(i, rows, lanes, value, x=x, ok=ok):
            mid_ext[i, x, rows, lanes] = jnp.where(ok, value, 0.0)

        collide_block(
            reads,
            lambda axis, rows, lanes, ref=ref: ref[19 + axis, rows, lanes],
            lambda rows, lanes, ref=ref: ref[22, rows, lanes] > 0.0,
            face_rows(0, sign)[1],
            keep,
        )

    for ref, mine, mine_slot, near, far, sign, ok, out in (
        (from_down, to_down, NEAR_UP, NEAR_DOWN, FAR_DOWN, -1, in_down, low_face),
        (from_up, to_up, NEAR_DOWN, NEAR_UP, FAR_UP, 1, in_up, high_face),
    ):
        for i in range(19):
            cx, cy, cz = VEL[i]
            if cy == 0:
                v = entry(ref, near[i])
            elif cy == sign:
                v = entry(ref, 14 + far[i])
            else:
                v = entry(mine, mine_slot[i])
            if cx:
                v = pltpu.roll(v, (-cx) % 16, 0)
            reads[i] = shift_z(v, cz)
        row = iota((8, 128), 0)

        def keep_row(i, rows, lanes, value, out=out, far=far, ok=ok):
            x = row + rows.start
            good = ok & ((x > 1) | in_left) & ((x < EX - 2) | in_right)
            out[far[i], rows, lanes] = jnp.where(good, value, 0.0)

        collide_block(
            reads,
            lambda axis, rows, lanes, ref=ref: entry(ref, 19 + axis)[rows, lanes],
            lambda rows, lanes, ref=ref: entry(ref, 22)[rows, lanes] > 0.0,
            face_rows(1, sign)[1],
            keep_row,
        )

    def mid_copy(x):
        return pltpu.make_async_copy(mid_ext.at[:, pl.ds(x + 2, 1)], middle.at[:, pl.ds(x, 1)], mid_sems.at[x])

    def first_copy(x):
        return pltpu.make_async_copy(first.at[:, pl.ds(x, 1)], initial.at[:, pl.ds(x, 1)], first_sems.at[x])

    def mid_plane(x, carry):
        for i in range(19):
            reads[i] = read_plane(ext, low_near, high_near, x + 2, i, NEAR_DOWN, NEAR_UP)

        def keep(i, rows, lanes, value):
            mid_ext[i, x + 2, rows, lanes] = value

        collide_block(
            reads,
            lambda axis, rows, lanes: vel_late[axis, x, rows, lanes],
            lambda rows, lanes: solid[x, rows, lanes] > 0,
            ALL,
            keep,
        )
        mid_copy(x).start()
        return carry

    lax.fori_loop(0, BX, mid_plane, 0)

    def first_plane(x, carry):
        for i in range(19):
            reads[i] = read_plane(mid_ext, low_face, high_face, x + 2, i, FAR_DOWN, FAR_UP)

        def keep(i, rows, lanes, value):
            first[i, x, rows, lanes] = value

        collide_block(
            reads,
            lambda axis, rows, lanes: vel_early[axis, x, rows, lanes],
            lambda rows, lanes: solid[x, rows, lanes] > 0,
            ALL,
            keep,
        )
        first_copy(x).start()
        return carry

    lax.fori_loop(0, BX, first_plane, 0)

    def finish(x, carry):
        mid_copy(x).wait()
        first_copy(x).wait()
        return carry

    lax.fori_loop(0, BX, finish, 0)


def shifted(value, axis, step):
    count = lax.axis_size(axis)
    return lax.ppermute(value, axis, [(i, (i + step) % count) for i in range(count)])


def body(adj_later, saved_pops, saved_scale, solid, seed_values, seed_contact, seed_cell):
    adj, pops, solid_h = in_hbm(adj_later), in_hbm(saved_pops), in_hbm(solid)
    scale = in_hbm(saved_scale.transpose(0, 2, 3, 4, 1).reshape(2, BX, 2 * BY, 19))
    block = pltpu.VMEM((24, 128), F32)
    x_face = pltpu.VMEM((24, BY, BZ), F32)
    y_face = pltpu.VMEM((Y_ROWS, BZ), F32)
    extended = pltpu.VMEM((19, EX, BY, BZ), F32)
    flow = pltpu.VMEM((3, BX, BY, BZ), F32)
    low, mid, high = call(
        group_items,
        (block,) * 3,
        [hbm] * 3,
        (in_hbm(seed_values.T), in_hbm(seed_contact.reshape(1, 128)), in_hbm(seed_cell.reshape(1, 128))),
        scratch=[
            pltpu.VMEM((24, 128), F32),
            pltpu.VMEM((19, 128), F32),
            pltpu.VMEM((1, 128), jnp.int32),
            pltpu.VMEM((1, 128), jnp.int32),
            pltpu.SemaphoreType.DMA((3,)),
        ],
    )
    below = in_vmem(shifted(high, "gy", 1))
    above = in_vmem(shifted(low, "gy", -1))

    raw = pltpu.VMEM((19, BX, BY, BZ), jnp.bfloat16)
    table = pltpu.VMEM((BX, 2 * BY, 19), F32)
    vel_late, ext, solid_v = call(
        late_velocities,
        (flow, extended, pltpu.VMEM((BX, BY, BZ), jnp.int32)),
        [hbm] * 4,
        (pops, scale, adj, solid_h),
        scratch=[raw, table, pltpu.SemaphoreType.DMA((5,))],
    )
    west, here, east = call(regroup, (block,) * 3, [vmem] * 4, (below, mid, above, solid_v))
    vel_early = call(
        early_velocities, flow, [hbm, hbm, vmem], (pops, scale, here),
        scratch=[raw, table, pltpu.SemaphoreType.DMA((3,))],
    )
    bf16 = jnp.bfloat16
    ext, to_left, to_right = call(
        own_seeds,
        (extended, x_face, x_face),
        [vmem] * 6,
        (ext, west, here, east, vel_late, solid_v),
        scratch=[pltpu.VMEM((128, 128), bf16), pltpu.VMEM((BZ, 128), bf16)],
        aliases={0: 0},
    )
    from_left = in_vmem(shifted(to_right, "gx", 1))
    from_right = in_vmem(shifted(to_left, "gx", -1))
    far_left = in_vmem(shifted(east, "gx", 2))
    far_right = in_vmem(shifted(west, "gx", -2))
    ext, to_down, to_up = call(
        y_faces,
        (extended, y_face, y_face),
        [vmem] * 9,
        (ext, from_left, from_right, far_left, far_right, west, east, vel_late, solid_v),
        scratch=[
            pltpu.VMEM((24, 256), F32), pltpu.VMEM((128, 256), bf16), pltpu.VMEM((BZ, 256), bf16),
            pltpu.VMEM((608, 256), bf16),
        ],
        aliases={0: 0},
    )
    from_down = in_vmem(shifted(to_up, "gy", 1))
    from_up = in_vmem(shifted(to_down, "gy", -1))
    field = jax.ShapeDtypeStruct((19, BX, BY, BZ), F32)
    return call(
        two_steps,
        (field, field),
        [vmem] * 10,
        (ext, from_left, from_right, from_down, from_up, to_down, to_up, vel_late, vel_early, solid_v),
        scratch=[
            pltpu.VMEM((19, EX, BY, BZ), F32),
            pltpu.VMEM((19, BX, BY, BZ), F32),
            pltpu.VMEM((14, 16, BZ), F32),
            pltpu.VMEM((14, 16, BZ), F32),
            pltpu.VMEM((5, 16, BZ), F32),
            pltpu.VMEM((5, 16, BZ), F32),
            pltpu.VMEM((19, BY, BZ), F32),
            pltpu.SemaphoreType.DMA((BX,)),
            pltpu.SemaphoreType.DMA((BX,)),
        ],
    )


def solution(mesh):
    return jax.shard_map(
        body,
        mesh=mesh,
        in_specs=(
            P(None, "gx", "gy", None),
            P(None, None, "gx", "gy", None),
            P(None, None, "gx", "gy", None),
            P("gx", "gy", None),
            P(("gx", "gy"), None),
            P(("gx", "gy"), None),
            P(("gx", "gy")),
        ),
        out_specs=(P(None, "gx", "gy", None), P(None, "gx", "gy", None)),
        check_vma=False,
    )
```

```python
import functools

import jax
import jax.numpy as jnp
from jax import lax
from jax.experimental import pallas as pl
from jax.experimental.pallas import tpu as pltpu
from jax.sharding import PartitionSpec as P

PAIRS = [
    (1, 2, (1, 0, 0)),
    (3, 4, (0, 1, 0)),
    (5, 6, (0, 0, 1)),
    (7, 8, (1, 1, 0)),
    (9, 10, (1, -1, 0)),
    (11, 12, (1, 0, 1)),
    (13, 14, (1, 0, -1)),
    (15, 16, (0, 1, 1)),
    (17, 18, (0, 1, -1)),
]
VEL = [(0, 0, 0)] * 19
for _p, _m, _c in PAIRS:
    VEL[_p] = _c
    VEL[_m] = tuple(-v for v in _c)
OPP = [0] * 19
for _p, _m, _c in PAIRS:
    OPP[_p], OPP[_m] = _m, _p
RELAX = 0.8
F32 = jnp.float32
BX, BY, BZ = 8, 16, 256
EX = 12
LIST = 32


def face_rows(axis, sign):
    near = [i for i in range(19) if VEL[i][axis] in (0, sign)]
    far = [i for i in range(19) if VEL[i][axis] == sign]
    return near, far


vmem = pl.BlockSpec(memory_space=pltpu.VMEM)
anyspace = pl.BlockSpec(memory_space=pl.ANY)


hbm = pl.BlockSpec(memory_space=pltpu.HBM)


def in_vmem(x):
    return pltpu.with_memory_space_constraint(x, pltpu.VMEM)


def in_hbm(x):
    return pltpu.with_memory_space_constraint(x, pltpu.HBM)


def call(body, out_shape, in_specs, args, scratch=(), aliases=None, limit=20 << 20):
    single = not isinstance(out_shape, (tuple, list))
    outs = (out_shape,) if single else tuple(out_shape)
    out_specs = tuple(vmem if isinstance(o, type(pltpu.VMEM((8, 128), F32))) else anyspace for o in outs)
    res = pl.pallas_call(
        body,
        out_shape=outs,
        in_specs=in_specs,
        out_specs=out_specs,
        scratch_shapes=list(scratch),
        input_output_aliases=aliases or {},
        compiler_params=pltpu.CompilerParams(vmem_limit_bytes=limit),
    )(*args)
    return res[0] if single else res


def iota(shape, dim):
    return lax.broadcasted_iota(jnp.int32, shape, dim)


NEAR_DOWN = {i: n for n, i in enumerate(face_rows(1, -1)[0])}
NEAR_UP = {i: n for n, i in enumerate(face_rows(1, 1)[0])}
FAR_DOWN = {i: n for n, i in enumerate(face_rows(1, -1)[1])}
FAR_UP = {i: n for n, i in enumerate(face_rows(1, 1)[1])}
ALL = list(range(19))


def plane_velocity(pop, store):
    density = pop(0)
    mom = [None, None, None]
    for plus, minus, c in PAIRS:
        fp, fm = pop(plus), pop(minus)
        density = density + (fp + fm)
        d = fp - fm
        for axis in range(3):
            if c[axis]:
                if mom[axis] is None:
                    mom[axis] = d
                elif c[axis] > 0:
                    mom[axis] = mom[axis] + d
                else:
                    mom[axis] = mom[axis] - d
    inv = 1.0 / density
    for axis in range(3):
        store(axis, mom[axis] * inv)


def group_items(values, contact, cell, low, mid, high, pay, own_values, own_contact, own_cell, sems):
    copies = [
        pltpu.make_async_copy(src, dst, sems.at[n])
        for n, (src, dst) in enumerate(((contact, own_contact), (cell, own_cell), (values, own_values)))
    ]
    for c in copies:
        c.start()
    for c in copies:
        c.wait()
    code = own_contact[...]
    hot = (iota((16, 128), 0) == code).astype(jnp.bfloat16)
    before = (iota((128, 128), 0) < iota((128, 128), 1)).astype(jnp.bfloat16)
    counts = jnp.dot(hot, before, preferred_element_type=F32)
    rank = jnp.sum(jnp.where(iota((16, 128), 0) == code, counts, 0.0), axis=0, keepdims=True).astype(jnp.int32)
    third = (code >= 3).astype(jnp.int32) + (code >= 6).astype(jnp.int32)
    slot = (code - 3 * third) * 128 + third * LIST + rank
    pay[...] = jnp.zeros((24, 128), F32)
    pay[0:19, :] = own_values[...]
    pay[19:20, :] = own_cell[...].astype(F32)
    payload = pay[...]
    for part, out in enumerate((low, mid, high)):
        pick = (iota((128, 128), 0) + 128 * part == slot).astype(F32)
        out[...] = lax.dot_general(
            payload, pick, (((1,), (1,)), ((), ())), precision=lax.Precision.HIGHEST, preferred_element_type=F32
        )


def velocity_planes(pops, scale, step, vel, raw, table_all, sems):
    scale_copy = pltpu.make_async_copy(scale.at[step], table_all, sems.at[0])
    scale_copy.start()
    copies = []
    for h in range(2):
        c = pltpu.make_async_copy(pops.at[step, :, pl.ds(4 * h, 4)], raw.at[:, pl.ds(4 * h, 4)], sems.at[1 + h])
        c.start()
        copies.append(c)
    yield
    scale_copy.wait()
    for h, c in enumerate(copies):
        c.wait()

        def plane(x, carry):
            for b in range(2):
                lanes = slice(128 * b, 128 * b + 128)
                table = table_all[x, pl.ds(b, BY, stride=2), :]

                def pop(i):
                    return raw[i, x, :, lanes].astype(F32) * jnp.broadcast_to(table[:, i : i + 1], (BY, 128))

                def store(axis, value):
                    vel[axis, x, :, lanes] = value

                plane_velocity(pop, store)
            return carry

        lax.fori_loop(4 * h, 4 * h + 4, plane, 0)
    yield


def late_velocities(pops, scale, adj, solid_in, vel, ext, solid, raw, table_all, sems):
    work = velocity_planes(pops, scale, 1, vel, raw, table_all, sems)
    next(work)
    adj_copy = pltpu.make_async_copy(adj, ext.at[:, pl.ds(2, BX)], sems.at[3])
    adj_copy.start()
    solid_copy = pltpu.make_async_copy(solid_in, solid, sems.at[4])
    solid_copy.start()
    next(work)
    adj_copy.wait()
    solid_copy.wait()


def early_velocities(pops, scale, after, vel, raw, table_all, sems):
    del after
    work = velocity_planes(pops, scale, 0, vel, raw, table_all, sems)
    next(work)
    next(work)


def regroup(below, own, above, after, west, here, east):
    del after
    gy = lax.axis_index("gy")
    a = jnp.where(gy > 0, below[...], 0.0)
    b = own[...]
    c = jnp.where(gy < lax.axis_size("gy") - 1, above[...], 0.0)
    lane = iota((24, 128), 1)
    for j, out in enumerate((west, here, east)):
        ra = pltpu.roll(a, (-LIST * j) % 128, 1)
        rb = pltpu.roll(b, (LIST - LIST * j) % 128, 1)
        rc = pltpu.roll(c, (2 * LIST - LIST * j) % 128, 1)
        out[...] = jnp.where(
            lane < LIST, ra, jnp.where(lane < 2 * LIST, rb, jnp.where(lane < 3 * LIST, rc, 0.0))
        )


Y_LEAD = 8
Y_HELD = BX + 2
Y_ROWS = Y_LEAD + 23 * Y_HELD + 10


def put(n, x, shift):
    row = Y_LEAD + Y_HELD * n + x - 1 - shift
    return slice(row, row + 1)


def entry(face, n, shift):
    first = Y_LEAD + Y_HELD * n - 1 - shift
    return face[first : first + 16, :]


def halves(v):
    hi = v.astype(jnp.bfloat16)
    return hi, (v - hi.astype(F32)).astype(jnp.bfloat16)


def one_hot(rows, targets):
    return (iota((rows, targets.shape[1]), 0) == targets).astype(F32).astype(jnp.bfloat16)


def contract_lanes(a, b):
    return lax.dot_general(a, b, (((1,), (1,)), ((), ())), preferred_element_type=F32)


def add_own(ext, items, where_xy, where_z):
    cell = items[19:20, :].astype(jnp.int32)
    where_xy[...] = one_hot(128, cell // BZ)
    where_z[...] = one_hot(BZ, cell % BZ)
    for i in range(19):
        hi, lo = halves(items[i : i + 1, :])
        rows = where_xy[...]
        field = contract_lanes(jnp.concatenate([rows * hi, rows * lo], axis=0), where_z[...])
        ext[i, 2 : 2 + BX] = ext[i, 2 : 2 + BX] + (field[0:128] + field[128:256]).reshape(BX, BY, BZ)


def own_seeds(ext_in, west, here, east, vel, solid, ext, to_left, to_right, where_xy, where_z):
    del ext_in
    add_own(ext, here, where_xy, where_z)
    for sign, out, items, near_x, far_x in ((1, to_left, west, 2, 3), (-1, to_right, east, 9, 8)):
        near, far = face_rows(0, sign)
        for slot, i in enumerate(near):
            out[slot] = ext[i, near_x]
        for slot, i in enumerate(far):
            out[14 + slot] = ext[i, far_x]
        for axis in range(3):
            out[19 + axis] = vel[axis, near_x - 2]
        out[22] = (solid[near_x - 2] > 0).astype(F32)
        out[23, :, 0:128] = items[0:16, :]
        out[23, 0:8, 128:256] = items[16:24, :]
        out[23, 8:16, 128:256] = jnp.zeros((8, 128), F32)


def halo_scatter(items, near_rows, near_target, far_rows, far_target, height, add, stack):
    near_hot, far_hot = one_hot(16, near_target), one_hot(16, far_target)
    entries = [(near_hot, i, 0) for i in near_rows] + [(far_hot, i, 1) for i in far_rows]
    count = len(entries)
    for n, (hot, i, deep) in enumerate(entries):
        hi, lo = halves(items[i : i + 1, :])
        stack[16 * n : 16 * n + 16, :] = hot * hi
        stack[16 * (count + n) : 16 * (count + n) + 16, :] = hot * lo
    field = contract_lanes(stack[...], one_hot(BZ, height))
    for n, (hot, i, deep) in enumerate(entries):
        add(i, deep, field[16 * n : 16 * n + 16] + field[16 * (count + n) : 16 * (count + n) + 16])


def y_faces(
    ext_in, from_left, from_right, far_left, far_right, west, east, vel, solid,
    ext, to_down, to_up,
    items, where_xy, where_z, stack,
):
    del ext_in
    gx, last = lax.axis_index("gx"), lax.axis_size("gx") - 1
    for n, (face, ok) in enumerate(((from_left, gx > 0), (from_right, gx < last))):
        lanes = slice(128 * n, 128 * n + 128)
        items[0:16, lanes] = jnp.where(ok, face[23, :, 0:128], 0.0)
        items[16:24, lanes] = jnp.where(ok, face[23, 0:8, 128:256], 0.0)
    add_own(ext, items, where_xy, where_z)
    for sign, ref, mine, other, ok, other_ok, near_x, far_x, near_cell in (
        (-1, from_left, west, far_left, gx > 0, gx > 1, 1, 0, BX - 1),
        (1, from_right, east, far_right, gx < last, gx < last - 1, 10, 11, 0),
    ):
        near, far = face_rows(0, sign)
        slots = {i: n for n, i in enumerate(near)}, {i: 14 + n for n, i in enumerate(far)}
        items[:, 0:128] = mine[...]
        items[:, 128:256] = jnp.where(other_ok, other[...], 0.0)
        cell = items[19:20, :].astype(jnp.int32)
        x, y = cell // (BY * BZ), (cell // BZ) % BY

        def add(i, deep, field, ref=ref, ok=ok, near_x=near_x, far_x=far_x, slots=slots):
            ext[i, far_x if deep else near_x] = jnp.where(ok, ref[slots[deep][i]] + field, 0.0)

        halo_scatter(
            items, near, jnp.where(x == near_cell, y, -1), far, jnp.where(x == near_cell + sign, y, -1),
            cell % BZ, add, stack,
        )
    for sign, out, near_y, far_y in ((1, to_down, 0, 1), (-1, to_up, BY - 1, BY - 2)):
        near, far = face_rows(1, sign)
        out[0:Y_LEAD, :] = jnp.zeros((Y_LEAD, BZ), F32)
        out[Y_ROWS - 10 : Y_ROWS, :] = jnp.zeros((10, BZ), F32)
        for base, pops, y in ((0, near, near_y), (14, far, far_y)):
            for slot, i in enumerate(pops):
                shift = VEL[i][0]
                for x in range(1 + shift, EX - 1 + shift):
                    out[put(base + slot, x, shift), :] = ext[i, x, y : y + 1, :]
        for row in range(19, 23):
            out[put(row, 1, 0), :] = from_left[row, near_y : near_y + 1, :]
            out[put(row, EX - 2, 0), :] = from_right[row, near_y : near_y + 1, :]
        for x in range(BX):
            for axis in range(3):
                out[put(19 + axis, x + 2, 0), :] = vel[axis, x, near_y : near_y + 1, :]
            out[put(22, x + 2, 0), :] = (solid[x, near_y : near_y + 1, :] > 0).astype(F32)


def adjoint_collide(u, is_solid, r, want):
    square = u[0] * u[0] + u[1] * u[1] + u[2] * u[2]
    axis_sum = diag_sum = axis_quad = diag_quad = None
    axis_mom = [None, None, None]
    diag_mom = [None, None, None]

    def plus(a, b):
        return b if a is None else a + b

    for n, (ip, im, c) in enumerate(PAIRS):
        s, d = r[ip] + r[im], r[ip] - r[im]
        p = None
        for axis in range(3):
            if c[axis]:
                p = u[axis] if p is None else (p + u[axis] if c[axis] > 0 else p - u[axis])
        q = p * s
        m = d + 3.0 * q
        if n < 3:
            axis_sum, axis_quad = plus(axis_sum, s), plus(axis_quad, q * p)
            axis_mom[n] = m
        else:
            diag_sum, diag_quad = plus(diag_sum, s), plus(diag_quad, q * p)
            for axis in range(3):
                if c[axis] > 0:
                    diag_mom[axis] = plus(diag_mom[axis], m)
                elif c[axis] < 0:
                    diag_mom[axis] = diag_mom[axis] - m
    scale = 1.0 / RELAX
    keep = 1.0 - scale
    total = (scale / 3.0) * r[0] + (scale / 18.0) * axis_sum + (scale / 36.0) * diag_sum
    quad = (4.5 * scale / 18.0) * axis_quad + (4.5 * scale / 36.0) * diag_quad
    density = total * (1.0 + 1.5 * square) - quad
    triple = 3.0 * total
    grad = [
        (3.0 * scale / 18.0) * axis_mom[a] + (3.0 * scale / 36.0) * diag_mom[a] - triple * u[a] for a in range(3)
    ]
    out = {}
    if 0 in want:
        out[0] = jnp.where(is_solid, r[0], keep * r[0] + density)
    for ip, im, c in PAIRS:
        if ip not in want and im not in want:
            continue
        g = None
        for axis in range(3):
            if c[axis]:
                g = grad[axis] if g is None else (g + grad[axis] if c[axis] > 0 else g - grad[axis])
        if ip in want:
            out[ip] = jnp.where(is_solid, r[im], keep * r[ip] + (density + g))
        if im in want:
            out[im] = jnp.where(is_solid, r[ip], keep * r[im] + (density - g))
    return out


def shift_z(v, step):
    if step == 0:
        return v
    lane = iota(v.shape, 1)
    if step > 0:
        return jnp.where(lane == BZ - 1, 0.0, pltpu.roll(v, BZ - 1, 1))
    return jnp.where(lane == 0, 0.0, pltpu.roll(v, 1, 1))


def read_plane(field, x, i, low_face=None, high_face=None):
    cx, cy, cz = VEL[i]
    v = field[i, x + cx]
    if cy:
        row = iota(v.shape, 0)
        if cy > 0:
            v = pltpu.roll(v, BY - 1, 0)
            if high_face is not None:
                edge = high_face[FAR_UP[i], pl.ds(x + cx, 1), :]
                v = jnp.where(row == BY - 1, jnp.broadcast_to(edge, v.shape), v)
        else:
            v = pltpu.roll(v, 1, 0)
            if low_face is not None:
                edge = low_face[FAR_DOWN[i], pl.ds(x + cx, 1), :]
                v = jnp.where(row == 0, jnp.broadcast_to(edge, v.shape), v)
    return shift_z(v, cz)


def collide_block(reads, load_u, load_solid, want, store):
    for h in range(2):
        for b in range(2):
            rows, lanes = slice(8 * h, 8 * h + 8), slice(128 * b, 128 * b + 128)
            r = [reads[i, rows, lanes] for i in range(19)]
            u = [load_u(axis, rows, lanes) for axis in range(3)]
            out = adjoint_collide(u, load_solid(rows, lanes), r, want)
            for i in want:
                store(i, rows, lanes, out[i])


def late_planes(ext, from_left, from_right, vel, solid, mid, reads):
    gx = lax.axis_index("gx")
    for x, ref, ok, sign in (
        (1, from_left, gx > 0, -1),
        (EX - 2, from_right, gx < lax.axis_size("gx") - 1, 1),
    ):
        for i in range(19):
            reads[i] = read_plane(ext, x, i)

        def keep(i, rows, lanes, value, x=x, ok=ok):
            mid[i, x, rows, lanes] = jnp.where(ok, value, 0.0)

        collide_block(
            reads,
            lambda axis, rows, lanes, ref=ref: ref[19 + axis, rows, lanes],
            lambda rows, lanes, ref=ref: ref[22, rows, lanes] > 0.0,
            face_rows(0, sign)[1],
            keep,
        )

    def plane(x, carry):
        for i in range(19):
            reads[i] = read_plane(ext, x + 2, i)

        def keep(i, rows, lanes, value):
            mid[i, x + 2, rows, lanes] = value

        collide_block(
            reads,
            lambda axis, rows, lanes: vel[axis, x, rows, lanes],
            lambda rows, lanes: solid[x, rows, lanes] > 0,
            ALL,
            keep,
        )
        return carry

    lax.fori_loop(0, BX, plane, 0)


def finish_steps(
    mid_in, from_down, from_up, to_down, to_up, vel, solid,
    initial, middle, mid,
    first, low_face, high_face, reads, mid_sem, first_sems,
):
    del mid_in
    gx, gy = lax.axis_index("gx"), lax.axis_index("gy")
    in_left, in_right = gx > 0, gx < lax.axis_size("gx") - 1
    in_down, in_up = gy > 0, gy < lax.axis_size("gy") - 1
    row = iota((8, 128), 0)

    for ref, mine, near, far, mine_near, mine_far, sign, ok, out, y in (
        (from_down, to_down, NEAR_DOWN, FAR_DOWN, NEAR_UP, FAR_UP, -1, in_down, low_face, 0),
        (from_up, to_up, NEAR_UP, FAR_UP, NEAR_DOWN, FAR_DOWN, 1, in_up, high_face, BY - 1),
    ):
        for inside in (False, True):
            for i in range(19):
                cx, cy, cz = VEL[i]
                if inside:
                    if cy == 0:
                        v = entry(mine, mine_near[i], cx)
                    elif cy == sign:
                        v = jnp.where(ok, entry(ref, near[i], cx), 0.0)
                    else:
                        v = entry(mine, 14 + mine_far[i], cx)
                elif cy == 0:
                    v = entry(ref, near[i], cx)
                elif cy == sign:
                    v = entry(ref, 14 + far[i], cx)
                else:
                    v = entry(mine, mine_near[i], cx)
                if cx:
                    v = pltpu.roll(v, (-cx) % 16, 0)
                reads[i] = shift_z(v, cz)

            def keep_face(i, rows, lanes, value, out=out, far=far, ok=ok):
                x = row + rows.start
                good = ok & ((x > 1) | in_left) & ((x < EX - 2) | in_right)
                out[far[i], rows, lanes] = jnp.where(good, value, 0.0)

            def keep_row(i, rows, lanes, value, y=y):
                for x in range(max(1, rows.start), min(EX - 1, rows.stop)):
                    one = value[x - rows.start : x - rows.start + 1, :]
                    if x == 1:
                        if VEL[i][0] != -1:
                            continue
                        one = jnp.where(in_left, one, 0.0)
                    elif x == EX - 2:
                        if VEL[i][0] != 1:
                            continue
                        one = jnp.where(in_right, one, 0.0)
                    mid[i, x, y : y + 1, lanes] = one

            source = mine if inside else ref
            collide_block(
                reads,
                lambda axis, rows, lanes, source=source: entry(source, 19 + axis, 0)[rows, lanes],
                lambda rows, lanes, source=source: entry(source, 22, 0)[rows, lanes] > 0.0,
                ALL if inside else face_rows(1, sign)[1],
                keep_row if inside else keep_face,
            )

    mid_copy = pltpu.make_async_copy(mid.at[:, pl.ds(2, BX)], middle, mid_sem)
    mid_copy.start()

    def first_copy(x):
        return pltpu.make_async_copy(first.at[:, pl.ds(x, 1)], initial.at[:, pl.ds(x, 1)], first_sems.at[x])

    def plane(x, carry):
        for i in range(19):
            reads[i] = read_plane(mid, x + 2, i, low_face, high_face)

        def keep(i, rows, lanes, value):
            first[i, x, rows, lanes] = value

        collide_block(
            reads,
            lambda axis, rows, lanes: vel[axis, x, rows, lanes],
            lambda rows, lanes: solid[x, rows, lanes] > 0,
            ALL,
            keep,
        )
        first_copy(x).start()
        return carry

    lax.fori_loop(0, BX, plane, 0)
    mid_copy.wait()

    def drain(x, carry):
        first_copy(x).wait()
        return carry

    lax.fori_loop(0, BX, drain, 0)


def shifted(value, axis, step):
    count = lax.axis_size(axis)
    return lax.ppermute(value, axis, [(i, (i + step) % count) for i in range(count)])


def body(adj_later, saved_pops, saved_scale, solid, seed_values, seed_contact, seed_cell):
    adj, pops, solid_h = in_hbm(adj_later), in_hbm(saved_pops), in_hbm(solid)
    scale = in_hbm(saved_scale.transpose(0, 2, 3, 4, 1).reshape(2, BX, 2 * BY, 19))
    block = pltpu.VMEM((24, 128), F32)
    x_face = pltpu.VMEM((24, BY, BZ), F32)
    y_face = pltpu.VMEM((Y_ROWS, BZ), F32)
    extended = pltpu.VMEM((19, EX, BY, BZ), F32)
    flow = pltpu.VMEM((3, BX, BY, BZ), F32)
    low, mid, high = call(
        group_items,
        (block,) * 3,
        [hbm] * 3,
        (in_hbm(seed_values.T), in_hbm(seed_contact.reshape(1, 128)), in_hbm(seed_cell.reshape(1, 128))),
        scratch=[
            pltpu.VMEM((24, 128), F32),
            pltpu.VMEM((19, 128), F32),
            pltpu.VMEM((1, 128), jnp.int32),
            pltpu.VMEM((1, 128), jnp.int32),
            pltpu.SemaphoreType.DMA((3,)),
        ],
    )
    below = in_vmem(shifted(high, "gy", 1))
    above = in_vmem(shifted(low, "gy", -1))

    raw = pltpu.VMEM((19, BX, BY, BZ), jnp.bfloat16)
    table = pltpu.VMEM((BX, 2 * BY, 19), F32)
    vel_late, ext, solid_v = call(
        late_velocities,
        (flow, extended, pltpu.VMEM((BX, BY, BZ), jnp.int32)),
        [hbm] * 4,
        (pops, scale, adj, solid_h),
        scratch=[raw, table, pltpu.SemaphoreType.DMA((5,))],
    )
    west, here, east = call(regroup, (block,) * 3, [vmem] * 4, (below, mid, above, solid_v))
    vel_early = call(
        early_velocities, flow, [hbm, hbm, vmem], (pops, scale, here),
        scratch=[raw, table, pltpu.SemaphoreType.DMA((3,))],
    )
    bf16 = jnp.bfloat16
    ext, to_left, to_right = call(
        own_seeds,
        (extended, x_face, x_face),
        [vmem] * 6,
        (ext, west, here, east, vel_late, solid_v),
        scratch=[pltpu.VMEM((128, 128), bf16), pltpu.VMEM((BZ, 128), bf16)],
        aliases={0: 0},
    )
    from_left = in_vmem(shifted(to_right, "gx", 1))
    from_right = in_vmem(shifted(to_left, "gx", -1))
    far_left = in_vmem(shifted(east, "gx", 2))
    far_right = in_vmem(shifted(west, "gx", -2))
    ext, to_down, to_up = call(
        y_faces,
        (extended, y_face, y_face),
        [vmem] * 9,
        (ext, from_left, from_right, far_left, far_right, west, east, vel_late, solid_v),
        scratch=[
            pltpu.VMEM((24, 256), F32), pltpu.VMEM((128, 256), bf16), pltpu.VMEM((BZ, 256), bf16),
            pltpu.VMEM((608, 256), bf16),
        ],
        aliases={0: 0},
    )
    from_down = in_vmem(shifted(to_up, "gy", 1))
    from_up = in_vmem(shifted(to_down, "gy", -1))
    reads = pltpu.VMEM((19, BY, BZ), F32)
    mid = call(
        late_planes, extended, [vmem] * 5, (ext, from_left, from_right, vel_late, solid_v), scratch=[reads]
    )
    field = jax.ShapeDtypeStruct((19, BX, BY, BZ), F32)
    initial, middle, _ = call(
        finish_steps,
        (field, field, extended),
        [vmem] * 7,
        (mid, from_down, from_up, to_down, to_up, vel_early, solid_v),
        scratch=[
            pltpu.VMEM((19, BX, BY, BZ), F32),
            pltpu.VMEM((5, 16, BZ), F32),
            pltpu.VMEM((5, 16, BZ), F32),
            reads,
            pltpu.SemaphoreType.DMA(()),
            pltpu.SemaphoreType.DMA((BX,)),
        ],
        aliases={0: 2},
    )
    return initial, middle


def solution(mesh):
    return jax.shard_map(
        body,
        mesh=mesh,
        in_specs=(
            P(None, "gx", "gy", None),
            P(None, None, "gx", "gy", None),
            P(None, None, "gx", "gy", None),
            P("gx", "gy", None),
            P(("gx", "gy"), None),
            P(("gx", "gy"), None),
            P(("gx", "gy")),
        ),
        out_specs=(P(None, "gx", "gy", None), P(None, "gx", "gy", None)),
        check_vma=False,
    )
```

```python
import functools

import jax
import jax.numpy as jnp
from jax import lax
from jax.experimental import pallas as pl
from jax.experimental.pallas import tpu as pltpu
from jax.sharding import PartitionSpec as P

PAIRS = [
    (1, 2, (1, 0, 0)),
    (3, 4, (0, 1, 0)),
    (5, 6, (0, 0, 1)),
    (7, 8, (1, 1, 0)),
    (9, 10, (1, -1, 0)),
    (11, 12, (1, 0, 1)),
    (13, 14, (1, 0, -1)),
    (15, 16, (0, 1, 1)),
    (17, 18, (0, 1, -1)),
]
VEL = [(0, 0, 0)] * 19
for _p, _m, _c in PAIRS:
    VEL[_p] = _c
    VEL[_m] = tuple(-v for v in _c)
OPP = [0] * 19
for _p, _m, _c in PAIRS:
    OPP[_p], OPP[_m] = _m, _p
RELAX = 0.8
F32 = jnp.float32
BX, BY, BZ = 8, 16, 256
EX = 12
LIST = 32


def face_rows(axis, sign):
    near = [i for i in range(19) if VEL[i][axis] in (0, sign)]
    far = [i for i in range(19) if VEL[i][axis] == sign]
    return near, far


vmem = pl.BlockSpec(memory_space=pltpu.VMEM)
anyspace = pl.BlockSpec(memory_space=pl.ANY)


hbm = pl.BlockSpec(memory_space=pltpu.HBM)


def in_vmem(x):
    return pltpu.with_memory_space_constraint(x, pltpu.VMEM)


def in_hbm(x):
    return pltpu.with_memory_space_constraint(x, pltpu.HBM)


def call(body, out_shape, in_specs, args, scratch=(), aliases=None, limit=20 << 20):
    single = not isinstance(out_shape, (tuple, list))
    outs = (out_shape,) if single else tuple(out_shape)
    out_specs = tuple(vmem if isinstance(o, type(pltpu.VMEM((8, 128), F32))) else anyspace for o in outs)
    res = pl.pallas_call(
        body,
        out_shape=outs,
        in_specs=in_specs,
        out_specs=out_specs,
        scratch_shapes=list(scratch),
        input_output_aliases=aliases or {},
        compiler_params=pltpu.CompilerParams(vmem_limit_bytes=limit),
    )(*args)
    return res[0] if single else res


def iota(shape, dim):
    return lax.broadcasted_iota(jnp.int32, shape, dim)


NEAR_DOWN = {i: n for n, i in enumerate(face_rows(1, -1)[0])}
NEAR_UP = {i: n for n, i in enumerate(face_rows(1, 1)[0])}
FAR_DOWN = {i: n for n, i in enumerate(face_rows(1, -1)[1])}
FAR_UP = {i: n for n, i in enumerate(face_rows(1, 1)[1])}
ALL = list(range(19))


def plane_velocity(pop, store):
    density = pop(0)
    mom = [None, None, None]
    for plus, minus, c in PAIRS:
        fp, fm = pop(plus), pop(minus)
        density = density + (fp + fm)
        d = fp - fm
        for axis in range(3):
            if c[axis]:
                if mom[axis] is None:
                    mom[axis] = d
                elif c[axis] > 0:
                    mom[axis] = mom[axis] + d
                else:
                    mom[axis] = mom[axis] - d
    inv = 1.0 / density
    for axis in range(3):
        store(axis, mom[axis] * inv)


def group_items(values, contact, cell, low, mid, high, pay, own_values, own_contact, own_cell, sems):
    copies = [
        pltpu.make_async_copy(src, dst, sems.at[n])
        for n, (src, dst) in enumerate(((contact, own_contact), (cell, own_cell), (values, own_values)))
    ]
    for c in copies:
        c.start()
    for c in copies:
        c.wait()
    code = own_contact[...]
    hot = (iota((16, 128), 0) == code).astype(jnp.bfloat16)
    before = (iota((128, 128), 0) < iota((128, 128), 1)).astype(jnp.bfloat16)
    counts = jnp.dot(hot, before, preferred_element_type=F32)
    rank = jnp.sum(jnp.where(iota((16, 128), 0) == code, counts, 0.0), axis=0, keepdims=True).astype(jnp.int32)
    third = (code >= 3).astype(jnp.int32) + (code >= 6).astype(jnp.int32)
    slot = (code - 3 * third) * 128 + third * LIST + rank
    pay[...] = jnp.zeros((24, 128), F32)
    pay[0:19, :] = own_values[...]
    pay[19:20, :] = own_cell[...].astype(F32)
    payload = pay[...]
    for part, out in enumerate((low, mid, high)):
        pick = (iota((128, 128), 0) + 128 * part == slot).astype(F32)
        out[...] = lax.dot_general(
            payload, pick, (((1,), (1,)), ((), ())), precision=lax.Precision.HIGHEST, preferred_element_type=F32
        )


def velocity_planes(pops, scale, step, vel, raw, table_all, sems):
    scale_copy = pltpu.make_async_copy(scale.at[step], table_all, sems.at[0])
    scale_copy.start()
    copies = []
    for h in range(2):
        c = pltpu.make_async_copy(pops.at[step, :, pl.ds(4 * h, 4)], raw.at[:, pl.ds(4 * h, 4)], sems.at[1 + h])
        c.start()
        copies.append(c)
    yield
    scale_copy.wait()
    for h, c in enumerate(copies):
        c.wait()

        def plane(x, carry):
            for b in range(2):
                lanes = slice(128 * b, 128 * b + 128)
                table = table_all[x, pl.ds(b, BY, stride=2), :]

                def pop(i):
                    return raw[i, x, :, lanes].astype(F32) * jnp.broadcast_to(table[:, i : i + 1], (BY, 128))

                def store(axis, value):
                    vel[axis, x, :, lanes] = value

                plane_velocity(pop, store)
            return carry

        lax.fori_loop(4 * h, 4 * h + 4, plane, 0)
    yield


def late_velocities(pops, scale, adj, solid_in, vel, ext, solid, raw, table_all, sems):
    work = velocity_planes(pops, scale, 1, vel, raw, table_all, sems)
    next(work)
    adj_copy = pltpu.make_async_copy(adj, ext.at[:, pl.ds(2, BX)], sems.at[3])
    adj_copy.start()
    solid_copy = pltpu.make_async_copy(solid_in, solid, sems.at[4])
    solid_copy.start()
    next(work)
    adj_copy.wait()
    solid_copy.wait()


def early_velocities(pops, scale, after, vel, raw, table_all, sems):
    del after
    work = velocity_planes(pops, scale, 0, vel, raw, table_all, sems)
    next(work)
    next(work)


def regroup(below, own, above, after, west, here, east):
    del after
    gy = lax.axis_index("gy")
    a = jnp.where(gy > 0, below[...], 0.0)
    b = own[...]
    c = jnp.where(gy < lax.axis_size("gy") - 1, above[...], 0.0)
    lane = iota((24, 128), 1)
    for j, out in enumerate((west, here, east)):
        ra = pltpu.roll(a, (-LIST * j) % 128, 1)
        rb = pltpu.roll(b, (LIST - LIST * j) % 128, 1)
        rc = pltpu.roll(c, (2 * LIST - LIST * j) % 128, 1)
        out[...] = jnp.where(
            lane < LIST, ra, jnp.where(lane < 2 * LIST, rb, jnp.where(lane < 3 * LIST, rc, 0.0))
        )


Y_LEAD = 8
Y_HELD = BX + 2
Y_ROWS = Y_LEAD + 23 * Y_HELD + 10
Y_SENT = Y_LEAD + 14 * Y_HELD + 12


def put(n, x, shift):
    row = Y_LEAD + Y_HELD * n + x - 1 - shift
    return slice(row, row + 1)


def entry(face, n, shift):
    first = Y_LEAD + Y_HELD * n - 1 - shift
    return face[first : first + 16, :]


def halves(v):
    hi = v.astype(jnp.bfloat16)
    return hi, (v - hi.astype(F32)).astype(jnp.bfloat16)


def one_hot(rows, targets):
    return (iota((rows, targets.shape[1]), 0) == targets).astype(F32).astype(jnp.bfloat16)


def contract_lanes(a, b):
    return lax.dot_general(a, b, (((1,), (1,)), ((), ())), preferred_element_type=F32)


def add_own(ext, items, where_xy, where_z):
    cell = items[19:20, :].astype(jnp.int32)
    where_xy[...] = one_hot(128, cell // BZ)
    where_z[...] = one_hot(BZ, cell % BZ)
    for i in range(19):
        hi, lo = halves(items[i : i + 1, :])
        rows = where_xy[...]
        field = contract_lanes(jnp.concatenate([rows * hi, rows * lo], axis=0), where_z[...])
        ext[i, 2 : 2 + BX] = ext[i, 2 : 2 + BX] + (field[0:128] + field[128:256]).reshape(BX, BY, BZ)


def own_seeds(ext_in, west, here, east, vel, solid, ext, to_left, to_right, where_xy, where_z):
    del ext_in
    add_own(ext, here, where_xy, where_z)
    for sign, out, items, near_x, far_x in ((1, to_left, west, 2, 3), (-1, to_right, east, 9, 8)):
        near, far = face_rows(0, sign)
        for slot, i in enumerate(near):
            out[slot] = ext[i, near_x]
        for slot, i in enumerate(far):
            out[14 + slot] = ext[i, far_x]
        for axis in range(3):
            out[19 + axis] = vel[axis, near_x - 2]
        out[22] = (solid[near_x - 2] > 0).astype(F32)
        out[23, :, 0:128] = items[0:16, :]
        out[23, 0:8, 128:256] = items[16:24, :]
        out[23, 8:16, 128:256] = jnp.zeros((8, 128), F32)


def halo_scatter(items, near_rows, near_target, far_rows, far_target, height, add, stack):
    near_hot, far_hot = one_hot(16, near_target), one_hot(16, far_target)
    entries = [(near_hot, i, 0) for i in near_rows] + [(far_hot, i, 1) for i in far_rows]
    count = len(entries)
    for n, (hot, i, deep) in enumerate(entries):
        hi, lo = halves(items[i : i + 1, :])
        stack[16 * n : 16 * n + 16, :] = hot * hi
        stack[16 * (count + n) : 16 * (count + n) + 16, :] = hot * lo
    field = contract_lanes(stack[...], one_hot(BZ, height))
    for n, (hot, i, deep) in enumerate(entries):
        add(i, deep, field[16 * n : 16 * n + 16] + field[16 * (count + n) : 16 * (count + n) + 16])


def y_faces(
    ext_in, from_left, from_right, far_left, far_right, west, east, vel, solid, after,
    ext, to_down, to_up, send_down, send_up,
    items, where_xy, where_z, stack, reads, part,
):
    del ext_in, after
    gx, last = lax.axis_index("gx"), lax.axis_size("gx") - 1
    for n, (face, ok) in enumerate(((from_left, gx > 0), (from_right, gx < last))):
        lanes = slice(128 * n, 128 * n + 128)
        items[0:16, lanes] = jnp.where(ok, face[23, :, 0:128], 0.0)
        items[16:24, lanes] = jnp.where(ok, face[23, 0:8, 128:256], 0.0)
    add_own(ext, items, where_xy, where_z)
    for sign, ref, mine, other, ok, other_ok, near_x, far_x, near_cell in (
        (-1, from_left, west, far_left, gx > 0, gx > 1, 1, 0, BX - 1),
        (1, from_right, east, far_right, gx < last, gx < last - 1, 10, 11, 0),
    ):
        near, far = face_rows(0, sign)
        slots = {i: n for n, i in enumerate(near)}, {i: 14 + n for n, i in enumerate(far)}
        items[:, 0:128] = mine[...]
        items[:, 128:256] = jnp.where(other_ok, other[...], 0.0)
        cell = items[19:20, :].astype(jnp.int32)
        x, y = cell // (BY * BZ), (cell // BZ) % BY

        def add(i, deep, field, ref=ref, ok=ok, near_x=near_x, far_x=far_x, slots=slots):
            ext[i, far_x if deep else near_x] = jnp.where(ok, ref[slots[deep][i]] + field, 0.0)

        halo_scatter(
            items, near, jnp.where(x == near_cell, y, -1), far, jnp.where(x == near_cell + sign, y, -1),
            cell % BZ, add, stack,
        )
    for sign, out, send, near_y, far_y in ((1, to_down, send_down, 0, 1), (-1, to_up, send_up, BY - 1, BY - 2)):
        near, far = face_rows(1, sign)
        out[0:Y_LEAD, :] = jnp.zeros((Y_LEAD, BZ), F32)
        out[Y_ROWS - 10 : Y_ROWS, :] = jnp.zeros((10, BZ), F32)
        for base, pops, y in ((0, near, near_y), (14, far, far_y)):
            for slot, i in enumerate(pops):
                shift = VEL[i][0]
                for x in range(1 + shift, EX - 1 + shift):
                    out[put(base + slot, x, shift), :] = ext[i, x, y : y + 1, :]
        for row in range(19, 23):
            out[put(row, 1, 0), :] = from_left[row, near_y : near_y + 1, :]
            out[put(row, EX - 2, 0), :] = from_right[row, near_y : near_y + 1, :]
        for x in range(BX):
            for axis in range(3):
                out[put(19 + axis, x + 2, 0), :] = vel[axis, x, near_y : near_y + 1, :]
            out[put(22, x + 2, 0), :] = (solid[x, near_y : near_y + 1, :] > 0).astype(F32)
        for i in range(19):
            cx, cy, cz = VEL[i]
            if cy == -sign:
                reads[i] = jnp.zeros((16, BZ), F32)
                continue
            v = entry(out, 14 + far.index(i) if cy else near.index(i), cx)
            if cx:
                v = pltpu.roll(v, (-cx) % 16, 0)
            reads[i] = shift_z(v, cz)

        def keep(i, rows, lanes, value, far=far):
            part[far.index(i), rows, lanes] = value

        collide_block(
            reads,
            lambda axis, rows, lanes, out=out: entry(out, 19 + axis, 0)[rows, lanes],
            lambda rows, lanes: jnp.zeros((8, 128), jnp.bool_),
            far,
            keep,
        )
        send[0:Y_LEAD, :] = jnp.zeros((Y_LEAD, BZ), F32)
        send[Y_SENT - 12 : Y_SENT, :] = jnp.zeros((12, BZ), F32)
        for slot, i in enumerate(far):
            first, source = Y_LEAD + Y_HELD * slot, Y_LEAD + Y_HELD * near.index(i)
            send[first : first + Y_HELD, :] = out[source : source + Y_HELD, :]
            first = Y_LEAD + Y_HELD * (5 + slot)
            send[first : first + Y_HELD, :] = part[slot, 1 : 1 + Y_HELD, :]
        first, source = Y_LEAD + Y_HELD * 10, Y_LEAD + Y_HELD * 19
        send[first : first + 4 * Y_HELD, :] = out[source : source + 4 * Y_HELD, :]


def adjoint_collide(u, is_solid, r, want):
    square = u[0] * u[0] + u[1] * u[1] + u[2] * u[2]
    axis_sum = diag_sum = axis_quad = diag_quad = None
    axis_mom = [None, None, None]
    diag_mom = [None, None, None]

    def plus(a, b):
        return b if a is None else a + b

    for n, (ip, im, c) in enumerate(PAIRS):
        s, d = r[ip] + r[im], r[ip] - r[im]
        p = None
        for axis in range(3):
            if c[axis]:
                p = u[axis] if p is None else (p + u[axis] if c[axis] > 0 else p - u[axis])
        q = p * s
        m = d + 3.0 * q
        if n < 3:
            axis_sum, axis_quad = plus(axis_sum, s), plus(axis_quad, q * p)
            axis_mom[n] = m
        else:
            diag_sum, diag_quad = plus(diag_sum, s), plus(diag_quad, q * p)
            for axis in range(3):
                if c[axis] > 0:
                    diag_mom[axis] = plus(diag_mom[axis], m)
                elif c[axis] < 0:
                    diag_mom[axis] = diag_mom[axis] - m
    scale = 1.0 / RELAX
    keep = 1.0 - scale
    total = (scale / 3.0) * r[0] + (scale / 18.0) * axis_sum + (scale / 36.0) * diag_sum
    quad = (4.5 * scale / 18.0) * axis_quad + (4.5 * scale / 36.0) * diag_quad
    density = total * (1.0 + 1.5 * square) - quad
    triple = 3.0 * total
    grad = [
        (3.0 * scale / 18.0) * axis_mom[a] + (3.0 * scale / 36.0) * diag_mom[a] - triple * u[a] for a in range(3)
    ]
    out = {}
    if 0 in want:
        out[0] = jnp.where(is_solid, r[0], keep * r[0] + density)
    for ip, im, c in PAIRS:
        if ip not in want and im not in want:
            continue
        g = None
        for axis in range(3):
            if c[axis]:
                g = grad[axis] if g is None else (g + grad[axis] if c[axis] > 0 else g - grad[axis])
        if ip in want:
            out[ip] = jnp.where(is_solid, r[im], keep * r[ip] + (density + g))
        if im in want:
            out[im] = jnp.where(is_solid, r[ip], keep * r[im] + (density - g))
    return out


def shift_z(v, step):
    if step == 0:
        return v
    lane = iota(v.shape, 1)
    if step > 0:
        return jnp.where(lane == BZ - 1, 0.0, pltpu.roll(v, BZ - 1, 1))
    return jnp.where(lane == 0, 0.0, pltpu.roll(v, 1, 1))


def read_plane(field, x, i, low_face=None, high_face=None):
    cx, cy, cz = VEL[i]
    v = field[i, x + cx]
    if cy:
        row = iota(v.shape, 0)
        if cy > 0:
            v = pltpu.roll(v, BY - 1, 0)
            if high_face is not None:
                edge = high_face[FAR_UP[i], pl.ds(x + cx, 1), :]
                v = jnp.where(row == BY - 1, jnp.broadcast_to(edge, v.shape), v)
        else:
            v = pltpu.roll(v, 1, 0)
            if low_face is not None:
                edge = low_face[FAR_DOWN[i], pl.ds(x + cx, 1), :]
                v = jnp.where(row == 0, jnp.broadcast_to(edge, v.shape), v)
    return shift_z(v, cz)


def collide_block(reads, load_u, load_solid, want, store):
    for h in range(2):
        for b in range(2):
            rows, lanes = slice(8 * h, 8 * h + 8), slice(128 * b, 128 * b + 128)
            r = [reads[i, rows, lanes] for i in range(19)]
            u = [load_u(axis, rows, lanes) for axis in range(3)]
            out = adjoint_collide(u, load_solid(rows, lanes), r, want)
            for i in want:
                store(i, rows, lanes, out[i])


def late_planes(ext, from_left, from_right, vel, solid, mid, reads):
    gx = lax.axis_index("gx")
    for x, ref, ok, sign in (
        (1, from_left, gx > 0, -1),
        (EX - 2, from_right, gx < lax.axis_size("gx") - 1, 1),
    ):
        for i in range(19):
            reads[i] = read_plane(ext, x, i)

        def keep(i, rows, lanes, value, x=x, ok=ok):
            mid[i, x, rows, lanes] = jnp.where(ok, value, 0.0)

        collide_block(
            reads,
            lambda axis, rows, lanes, ref=ref: ref[19 + axis, rows, lanes],
            lambda rows, lanes, ref=ref: ref[22, rows, lanes] > 0.0,
            face_rows(0, sign)[1],
            keep,
        )

    def plane(x, carry):
        for i in range(19):
            reads[i] = read_plane(ext, x + 2, i)

        def keep(i, rows, lanes, value):
            mid[i, x + 2, rows, lanes] = value

        collide_block(
            reads,
            lambda axis, rows, lanes: vel[axis, x, rows, lanes],
            lambda rows, lanes: solid[x, rows, lanes] > 0,
            ALL,
            keep,
        )
        return carry

    lax.fori_loop(0, BX, plane, 0)


def finish_steps(
    mid_in, from_down, from_up, to_down, to_up, vel, solid,
    initial, middle, mid,
    first, low_face, high_face, reads, mid_sem, first_sems,
):
    del mid_in
    gx, gy = lax.axis_index("gx"), lax.axis_index("gy")
    in_left, in_right = gx > 0, gx < lax.axis_size("gx") - 1
    in_down, in_up = gy > 0, gy < lax.axis_size("gy") - 1
    row = iota((8, 128), 0)

    for ref, mine, far, mine_near, mine_far, sign, ok, out, y in (
        (from_down, to_down, FAR_DOWN, NEAR_UP, FAR_UP, -1, in_down, low_face, 0),
        (from_up, to_up, FAR_UP, NEAR_DOWN, FAR_DOWN, 1, in_up, high_face, BY - 1),
    ):
        for inside in (False, True):
            for i in range(19):
                cx, cy, cz = VEL[i]
                if inside and cy == 0:
                    v = entry(mine, mine_near[i], cx)
                elif inside and cy == sign:
                    v = jnp.where(ok, entry(ref, far[i], cx), 0.0)
                elif inside:
                    v = entry(mine, 14 + mine_far[i], cx)
                elif cy == -sign:
                    v = entry(mine, mine_near[i], cx)
                else:
                    reads[i] = jnp.zeros((16, BZ), F32)
                    continue
                if cx:
                    v = pltpu.roll(v, (-cx) % 16, 0)
                reads[i] = shift_z(v, cz)

            def keep_face(i, rows, lanes, value, ref=ref, out=out, far=far, ok=ok):
                x = row + rows.start
                sent = entry(ref, 5 + far[i], 0)[rows, lanes]
                value = value + jnp.where(entry(ref, 13, 0)[rows, lanes] > 0.0, 0.0, sent)
                good = ok & ((x > 1) | in_left) & ((x < EX - 2) | in_right)
                out[far[i], rows, lanes] = jnp.where(good, value, 0.0)

            def keep_row(i, rows, lanes, value, y=y):
                for x in range(max(1, rows.start), min(EX - 1, rows.stop)):
                    one = value[x - rows.start : x - rows.start + 1, :]
                    if x == 1:
                        if VEL[i][0] != -1:
                            continue
                        one = jnp.where(in_left, one, 0.0)
                    elif x == EX - 2:
                        if VEL[i][0] != 1:
                            continue
                        one = jnp.where(in_right, one, 0.0)
                    mid[i, x, y : y + 1, lanes] = one

            source, first_entry = (mine, 19) if inside else (ref, 10)
            collide_block(
                reads,
                lambda axis, rows, lanes, source=source, n=first_entry: entry(source, n + axis, 0)[rows, lanes],
                lambda rows, lanes, source=source, n=first_entry: entry(source, n + 3, 0)[rows, lanes] > 0.0,
                ALL if inside else face_rows(1, sign)[1],
                keep_row if inside else keep_face,
            )

    mid_copy = pltpu.make_async_copy(mid.at[:, pl.ds(2, BX)], middle, mid_sem)
    mid_copy.start()

    def first_copy(x):
        return pltpu.make_async_copy(first.at[:, pl.ds(x, 1)], initial.at[:, pl.ds(x, 1)], first_sems.at[x])

    def plane(x, carry):
        for i in range(19):
            reads[i] = read_plane(mid, x + 2, i, low_face, high_face)

        def keep(i, rows, lanes, value):
            first[i, x, rows, lanes] = value

        collide_block(
            reads,
            lambda axis, rows, lanes: vel[axis, x, rows, lanes],
            lambda rows, lanes: solid[x, rows, lanes] > 0,
            ALL,
            keep,
        )
        first_copy(x).start()
        return carry

    lax.fori_loop(0, BX, plane, 0)
    mid_copy.wait()

    def drain(x, carry):
        first_copy(x).wait()
        return carry

    lax.fori_loop(0, BX, drain, 0)


def shifted(value, axis, step):
    count = lax.axis_size(axis)
    return lax.ppermute(value, axis, [(i, (i + step) % count) for i in range(count)])


def body(adj_later, saved_pops, saved_scale, solid, seed_values, seed_contact, seed_cell):
    adj, pops, solid_h = in_hbm(adj_later), in_hbm(saved_pops), in_hbm(solid)
    scale = in_hbm(saved_scale.transpose(0, 2, 3, 4, 1).reshape(2, BX, 2 * BY, 19))
    block = pltpu.VMEM((24, 128), F32)
    x_face = pltpu.VMEM((24, BY, BZ), F32)
    y_face = pltpu.VMEM((Y_ROWS, BZ), F32)
    extended = pltpu.VMEM((19, EX, BY, BZ), F32)
    flow = pltpu.VMEM((3, BX, BY, BZ), F32)
    low, mid, high = call(
        group_items,
        (block,) * 3,
        [hbm] * 3,
        (in_hbm(seed_values.T), in_hbm(seed_contact.reshape(1, 128)), in_hbm(seed_cell.reshape(1, 128))),
        scratch=[
            pltpu.VMEM((24, 128), F32),
            pltpu.VMEM((19, 128), F32),
            pltpu.VMEM((1, 128), jnp.int32),
            pltpu.VMEM((1, 128), jnp.int32),
            pltpu.SemaphoreType.DMA((3,)),
        ],
    )
    below = in_vmem(shifted(high, "gy", 1))
    above = in_vmem(shifted(low, "gy", -1))

    raw = pltpu.VMEM((19, BX, BY, BZ), jnp.bfloat16)
    table = pltpu.VMEM((BX, 2 * BY, 19), F32)
    vel_late, ext, solid_v = call(
        late_velocities,
        (flow, extended, pltpu.VMEM((BX, BY, BZ), jnp.int32)),
        [hbm] * 4,
        (pops, scale, adj, solid_h),
        scratch=[raw, table, pltpu.SemaphoreType.DMA((5,))],
    )
    west, here, east = call(regroup, (block,) * 3, [vmem] * 4, (below, mid, above, solid_v))
    vel_early = call(
        early_velocities, flow, [hbm, hbm, vmem], (pops, scale, here),
        scratch=[raw, table, pltpu.SemaphoreType.DMA((3,))],
    )
    bf16 = jnp.bfloat16
    ext, to_left, to_right = call(
        own_seeds,
        (extended, x_face, x_face),
        [vmem] * 6,
        (ext, west, here, east, vel_late, solid_v),
        scratch=[pltpu.VMEM((128, 128), bf16), pltpu.VMEM((BZ, 128), bf16)],
        aliases={0: 0},
    )
    from_left = in_vmem(shifted(to_right, "gx", 1))
    from_right = in_vmem(shifted(to_left, "gx", -1))
    far_left = in_vmem(shifted(east, "gx", 2))
    far_right = in_vmem(shifted(west, "gx", -2))
    y_message = pltpu.VMEM((Y_SENT, BZ), F32)
    reads = pltpu.VMEM((19, BY, BZ), F32)
    ext, to_down, to_up, send_down, send_up = call(
        y_faces,
        (extended, y_face, y_face, y_message, y_message),
        [vmem] * 10,
        (ext, from_left, from_right, far_left, far_right, west, east, vel_late, solid_v, vel_early),
        scratch=[
            pltpu.VMEM((24, 256), F32), pltpu.VMEM((128, 256), bf16), pltpu.VMEM((BZ, 256), bf16),
            pltpu.VMEM((608, 256), bf16), reads, pltpu.VMEM((5, 16, BZ), F32),
        ],
        aliases={0: 0},
    )
    from_down = in_vmem(shifted(send_up, "gy", 1))
    from_up = in_vmem(shifted(send_down, "gy", -1))
    mid = call(
        late_planes, extended, [vmem] * 5, (ext, from_left, from_right, vel_late, solid_v), scratch=[reads]
    )
    field = jax.ShapeDtypeStruct((19, BX, BY, BZ), F32)
    initial, middle, _ = call(
        finish_steps,
        (field, field, extended),
        [vmem] * 7,
        (mid, from_down, from_up, to_down, to_up, vel_early, solid_v),
        scratch=[
            pltpu.VMEM((19, BX, BY, BZ), F32),
            pltpu.VMEM((5, 16, BZ), F32),
            pltpu.VMEM((5, 16, BZ), F32),
            reads,
            pltpu.SemaphoreType.DMA(()),
            pltpu.SemaphoreType.DMA((BX,)),
        ],
        aliases={0: 2},
    )
    return initial, middle


def solution(mesh):
    return jax.shard_map(
        body,
        mesh=mesh,
        in_specs=(
            P(None, "gx", "gy", None),
            P(None, None, "gx", "gy", None),
            P(None, None, "gx", "gy", None),
            P("gx", "gy", None),
            P(("gx", "gy"), None),
            P(("gx", "gy"), None),
            P(("gx", "gy")),
        ),
        out_specs=(P(None, "gx", "gy", None), P(None, "gx", "gy", None)),
        check_vma=False,
    )
```
